128 devices in a mesh: ctx: 32 (over x, y_hi, z), head: 4 (over y_lo, core).
Axes of the slice: x: 4, y: 4 (y_hi: 2, y_lo: 2; y = y_hi * 2 + y_lo), z: 4, core: 2. Of those that a mesh axis runs over, the one named last changes fastest.
Arguments:
- queries: bfloat16 [4096, 4096], P('ctx', 'head'), may hold values from -6 to 6
- keys_new: bfloat16 [4096, 1024], P('ctx', 'head'), may hold values from -6 to 6
- values_new: bfloat16 [4096, 1024], P('ctx', 'head'), may hold values from -6 to 6
- cache_keys: bfloat16 [32768, 1024], P('ctx', 'head'), may hold values from -6 to 6
- cache_values: bfloat16 [32768, 1024], P('ctx', 'head'), may hold values from -6 to 6
- block_list: int32 [8, 32, 64], P('head', 'ctx'), may hold values from -1 to 255, as said below
- block_count: int32 [8, 32], P('head', 'ctx'), may hold values from 0 to 64
- out_weight: bfloat16 [4096, 4096], P('head'), may hold values from -0.21875 to 0.21875
Outputs:
- mixed: bfloat16 [4096, 4096], P(('ctx', 'head'))
The draws below stay inside these ranges and needn't reach their ends.
Inputs may be any that keep to these rules, and one draw needn't show every extreme that they name: `block_list`: row (h, q) holds distinct cache block numbers in increasing order in its first block_count[h, q] entries and -1 after them. For each KV head, the query blocks of one aligned run of 1 query block together list at most 2 blocks of each aligned run of 8 cache blocks and at least one; for every KV head some run lists exactly 2 of every run of cache blocks.
All inputs are finite; a program needn't handle non-finite values.
Results may differ from the reference program's by a relative error of at most 0.015.
Values may be sent and summed in bfloat16 or wider, within the bound.
No kernel may reach another device: no remote copies, remote signals or barrier semaphores. Data moves between devices by JAX's collectives and lax.ppermute only.
A program may use at most 192 MiB of HBM per device.

```python
import jax
import jax.numpy as jnp
from jax import lax

D = 4096
HEADS = 32
KVH = 8
HD = 128
BLOCK = 128
CAP = 2
CB_DEV = 8
ROWS_DEV = 128
TOKENS = 4096
CACHE = 32768
QBLOCKS = 32
NBLOCKS = 256
SEL = 64


def block_choice(key):
    base_key = jax.random.fold_in(key, 11)
    split_keys = jax.random.split(base_key, 5)
    owners = NBLOCKS // CB_DEV
    qb_dev = ROWS_DEV // BLOCK
    taken_count = jax.random.randint(split_keys[0], (KVH, owners, owners), 1, CAP + 1)
    full_device = jax.random.randint(split_keys[1], (KVH,), 0, owners)
    is_full = jnp.arange(owners)[None, :] == full_device[:, None]
    taken_count = jnp.where(is_full[:, :, None], CAP, taken_count)
    scores = jax.random.randint(split_keys[2], (KVH, owners, owners, CB_DEV), 0, 1 << 20) * CB_DEV + jnp.arange(CB_DEV)
    block_rank = jnp.argsort(jnp.argsort(scores, axis=-1), axis=-1)
    union_mask = (block_rank < taken_count[..., None]).reshape(KVH, owners, NBLOCKS)
    levels = jax.random.randint(split_keys[3], (KVH, owners, qb_dev), 1, 9)
    first_block = (jnp.arange(qb_dev) == 0)[None, None, :]
    levels = jnp.where(is_full[:, :, None] & first_block, 8, levels)
    coin_flip = jax.random.randint(split_keys[4], (KVH, owners, qb_dev, NBLOCKS), 0, 8) < levels[..., None]
    block_ids = jnp.arange(NBLOCKS)
    covered = block_ids[None, :] % qb_dev == jnp.arange(qb_dev)[:, None]
    listed = (union_mask[:, :, None, :] & (coin_flip | covered[None, None])).reshape(KVH, QBLOCKS, NBLOCKS)
    counts = jnp.sum(listed.astype(jnp.int32), axis=-1).astype(jnp.int32)
    ordering = jnp.argsort(jnp.where(listed, block_ids, NBLOCKS + block_ids), axis=-1)
    leading = ordering[..., :SEL].astype(jnp.int32)
    slot_ids = jnp.arange(SEL)
    block_rows = jnp.where(slot_ids[None, None, :] < counts[..., None], leading, -1).astype(jnp.int32)
    return (block_rows, counts)


def draw_block_list(key, part):
    return block_choice(key)[0]


def draw_block_count(key, part):
    return block_choice(key)[1]


def draw_queries(key, part):
    result = jnp.clip(2.0 * jax.random.normal(jax.random.fold_in(key, 1), (TOKENS, HEADS * HD)), -6.0, 6.0)
    return result.astype(jnp.bfloat16)


def draw_keys_new(key, part):
    result = jnp.clip(jax.random.normal(jax.random.fold_in(key, 2), (TOKENS, KVH * HD)), -6.0, 6.0)
    return result.astype(jnp.bfloat16)


def block_levels(own_key, shape, pieces, smallest, largest):
    level = 1.0
    for dim, parts in pieces:
        heights = jax.random.uniform(jax.random.fold_in(jax.random.fold_in(own_key, 6), dim), (parts,), jnp.float32, smallest / len(pieces), largest / len(pieces))
        level = level * jnp.repeat(jnp.exp(heights), shape[dim] // parts).reshape((-1,) + (1,) * (len(shape) - 1 - dim))
    return level


def normal_values(own_key, shape, deviation, limit, shards=(), held_as=jnp.bfloat16):
    factor_of = block_levels(own_key, shape, shards, -0.22, 0.18) if shards else 1.0
    array = jax.random.normal(own_key, shape, jnp.float32) * deviation * factor_of
    return jnp.minimum(jnp.maximum(array, -limit), limit).astype(held_as)


def setup_inputs(seed: int = 0) -> dict:
    seeds = jax.random.split(jax.random.key(seed), 9)
    return {
        "queries": draw_queries(jax.random.fold_in(seeds[8], 71), 0),
        "keys_new": draw_keys_new(jax.random.fold_in(seeds[8], 71), 0),
        "values_new": normal_values(seeds[2], (TOKENS, KVH * HD), 1.0, 6.0, ((0, 32), (1, 4))),
        "cache_keys": normal_values(seeds[3], (CACHE, KVH * HD), 1.0, 6.0, ((0, 32), (1, 4))),
        "cache_values": normal_values(seeds[4], (CACHE, KVH * HD), 1.0, 6.0, ((0, 32), (1, 4))),
        "block_list": draw_block_list(jax.random.fold_in(seeds[8], 71), 0),
        "block_count": draw_block_count(jax.random.fold_in(seeds[8], 71), 0),
        "out_weight": normal_values(seeds[7], (HEADS * HD, D), (HEADS * HD // 6) ** -0.5, 0.21875, ((0, 4),)),
    }


def reference(queries, keys_new, values_new, cache_keys, cache_values, block_list, block_count, out_weight):
    nblocks = CACHE // BLOCK
    qblocks = TOKENS // BLOCK
    group_size = HEADS // KVH
    list_width = block_list.shape[2]
    cache_heads = cache_keys.reshape(nblocks, BLOCK, KVH, HD).transpose(2, 0, 1, 3)
    value_heads = cache_values.reshape(nblocks, BLOCK, KVH, HD).transpose(2, 0, 1, 3)
    stretch_keys = keys_new.reshape(qblocks, BLOCK, KVH, HD).transpose(2, 0, 1, 3)
    stretch_values = values_new.reshape(qblocks, BLOCK, KVH, HD).transpose(2, 0, 1, 3)
    query_blocks = queries.reshape(qblocks, BLOCK, KVH, group_size, HD)
    causal = jnp.arange(BLOCK)[:, None] >= jnp.arange(BLOCK)[None, :]
    score_scale = HD ** -0.5

    def one_block(block_index):
        block_rows = lax.dynamic_index_in_dim(block_list, block_index, 1, keepdims=False)
        counts = lax.dynamic_index_in_dim(block_count, block_index, 1, keepdims=False)
        in_use = jnp.arange(list_width)[None, :] < counts[:, None]
        safe_ids = jnp.where(in_use, block_rows, 0).astype(jnp.int32)
        key_rows = jax.vmap(lambda table, chosen: table[chosen])(cache_heads, safe_ids).reshape(KVH, list_width * BLOCK, HD)
        value_rows = jax.vmap(lambda table, chosen: table[chosen])(value_heads, safe_ids).reshape(KVH, list_width * BLOCK, HD)
        prev_block = jnp.maximum(block_index - 1, 0).astype(jnp.int32)
        prev_keys = lax.dynamic_index_in_dim(stretch_keys, prev_block, 1, keepdims=False)
        prev_values = lax.dynamic_index_in_dim(stretch_values, prev_block, 1, keepdims=False)
        own_keys = lax.dynamic_index_in_dim(stretch_keys, block_index, 1, keepdims=False)
        own_values = lax.dynamic_index_in_dim(stretch_values, block_index, 1, keepdims=False)
        all_keys = jnp.concatenate([key_rows, prev_keys, own_keys], axis=1).astype(jnp.float32)
        all_values = jnp.concatenate([value_rows, prev_values, own_values], axis=1).astype(jnp.float32)
        cache_ok = jnp.broadcast_to(jnp.repeat(in_use, BLOCK, axis=1)[:, None, :], (KVH, BLOCK, list_width * BLOCK))
        prev_ok = jnp.broadcast_to(block_index > 0, (KVH, BLOCK, BLOCK))
        own_ok = jnp.broadcast_to(causal, (KVH, BLOCK, BLOCK))
        allowed = jnp.concatenate([cache_ok, prev_ok, own_ok], axis=2)
        query_rows = lax.dynamic_index_in_dim(query_blocks, block_index, 0, keepdims=False).transpose(1, 2, 0, 3).astype(jnp.float32)
        scores = jnp.einsum('hgrd,hkd->hgrk', query_rows, all_keys) * score_scale
        scores = jnp.where(allowed[:, None], scores, -jnp.inf)
        row_max = jnp.max(scores, axis=-1, keepdims=True)
        weights = jnp.exp(scores - row_max)
        weight_sum = jnp.sum(weights, axis=-1, keepdims=True)
        rounded = lax.optimization_barrier(weights.astype(jnp.bfloat16)).astype(jnp.float32)
        mixture = jnp.einsum('hgrk,hkd->hgrd', rounded, all_values) / weight_sum
        return mixture.astype(jnp.bfloat16).transpose(2, 0, 1, 3).reshape(BLOCK, KVH * group_size * HD)

    attention = lax.map(one_block, jnp.arange(qblocks, dtype=jnp.int32)).reshape(TOKENS, HEADS * HD)
    return jnp.dot(attention, out_weight, preferred_element_type=jnp.float32).astype(jnp.bfloat16)
```

```python
import functools

import jax
import jax.numpy as jnp
from jax import lax
from jax.experimental import pallas as pl
from jax.experimental.pallas import tpu as pltpu
from jax.sharding import PartitionSpec as P

HD = 128
BLOCK = 128
CB_DEV = 8
KVL = 2
GROUP = 4
NX, NY, NZ = 4, 2, 4
HALVES, CORES = 2, 2
COLS = GROUP * BLOCK
ROWS = HD + 8
STEPS = (1, -1, 2)
LOG2E = 1.4426950408889634
CEXP = LOG2E * HD**-0.5
NEG = -1e30
AXES = ("ctx", "head")
BF = jnp.bfloat16
F32 = jnp.float32


def flat(x, y, z, yl, c):
    return ((x * NY + y) * NZ + z) * (HALVES * CORES) + yl * CORES + c


def everyone():
    for x in range(NX):
        for y in range(NY):
            for z in range(NZ):
                for yl in range(HALVES):
                    for c in range(CORES):
                        yield x, y, z, yl, c


def moved(x, y, z, yl, c, by, keys):
    if (c == 0) == keys:
        return flat(x, y, (z + by) % NZ, yl, c)
    return flat((x + by) % NX, y, z, yl, c)


def pairs_along(by, keys):
    return [(flat(*d), moved(*d, by, keys)) for d in everyone()]


PAIRS_Y = [(flat(x, y, z, l, c), flat(x, 1 - y, z, l, c)) for x, y, z, l, c in everyone()]
PAIRS_CORE = [(flat(x, y, z, l, c), flat(x, y, z, l, 1 - c)) for x, y, z, l, c in everyone()]
PAIRS_LO = [(flat(x, y, z, l, c), flat(x, y, z, 1 - l, c)) for x, y, z, l, c in everyone()]
PAIRS_PREV = [
    (i * HALVES * CORES + h, (i + 1) * HALVES * CORES + h)
    for i in range(NX * NY * NZ - 1)
    for h in range(HALVES * CORES)
]


def send(array, pairs):
    return lax.ppermute(array, AXES, pairs)


def nt(a, b):
    return lax.dot_general(a, b, (((1,), (1,)), ((), ())), preferred_element_type=F32)


def nn(a, b):
    return lax.dot_general(a, b, (((1,), (0,)), ((), ())), preferred_element_type=F32)


def turned(block):
    return block.astype(F32).T.astype(BF)


def packed_sum(level):
    hi = level.astype(BF)
    rest = level - hi.astype(F32)
    mid = rest.astype(BF)
    low = (rest - mid.astype(F32)).astype(BF)
    return jnp.concatenate([hi.astype(F32), mid.astype(F32), low.astype(F32), jnp.zeros((5, COLS), F32)], axis=0).astype(BF)


def pack_kernel(k_ref, v_ref, o_ref):
    for h in range(KVL):
        for b in range(CB_DEV):
            rows, cols = slice(b * BLOCK, (b + 1) * BLOCK), slice(h * HD, (h + 1) * HD)
            o_ref[h, b, 0] = k_ref[rows, cols]
            o_ref[h, b, 1] = turned(v_ref[rows, cols])


def query_rows(q):
    return jnp.concatenate([q[:, m * HD : (m + 1) * HD] for m in range(GROUP)], axis=0)


def attend_kernel(tab_ref, q_ref, *refs):
    kvs, o_ref = refs[:-1], refs[-1]
    for y in range(NY):
        for h in range(KVL):
            q = query_rows(q_ref[y, 0:BLOCK, h * COLS : (h + 1) * COLS])
            scores, offs, values = [], [], []
            for s, kv in enumerate(kvs):
                first, second = tab_ref[y, h, s, 0], tab_ref[y, h, s, 1]
                for j, b in enumerate((first, second)):
                    scores.append(nt(kv[h, b, 0], q))
                    values.append(kv[h, b, 1])
                    offs.append(None if j == 0 else jnp.where(second == first, NEG, 0.0).astype(F32))
            tops = [
                jnp.max(t, axis=0, keepdims=True) if o is None else jnp.max(t, axis=0, keepdims=True) + o
                for t, o in zip(scores, offs)
            ]
            top = functools.reduce(jnp.maximum, tops) * CEXP
            total = jnp.zeros((1, COLS), F32)
            weights = []
            for t, o in zip(scores, offs):
                w = jnp.exp2(t * CEXP - (top if o is None else top - o))
                total = total + jnp.sum(w, axis=0, keepdims=True)
                weights.append(w.astype(BF))
            mixture = nn(jnp.concatenate(values, axis=1), jnp.concatenate(weights, axis=0))
            o_ref[y, h, 0:HD, :] = (mixture * (1.0 / total)).astype(BF)
            o_ref[y, h, HD:ROWS, :] = packed_sum(top + jnp.log(total) * LOG2E)


def stretch_kernel(first_ref, q_ref, k_ref, v_ref, prev_ref, o_ref, l_ref):
    off = jnp.where(first_ref[0] == 0, NEG, 0.0).astype(F32)
    key = lax.broadcasted_iota(jnp.int32, (BLOCK, COLS), 0)
    row = lax.broadcasted_iota(jnp.int32, (BLOCK, COLS), 1) % BLOCK
    for h in range(KVL):
        q = query_rows(q_ref[:, h * COLS : (h + 1) * COLS])
        cols = slice(h * HD, (h + 1) * HD)
        vcols = slice((KVL + h) * HD, (KVL + h + 1) * HD)
        own = jnp.where(key <= row, nt(k_ref[:, cols], q), NEG)
        before = nt(prev_ref[:, cols], q)
        top = jnp.maximum(
            jnp.max(own, axis=0, keepdims=True), jnp.max(before, axis=0, keepdims=True) + off
        ) * CEXP
        w_own = jnp.exp2(own * CEXP - top)
        w_before = jnp.exp2(before * CEXP - (top - off))
        total = jnp.sum(w_own, axis=0, keepdims=True) + jnp.sum(w_before, axis=0, keepdims=True)
        mixture = nn(turned(v_ref[:, cols]), w_own.astype(BF)) + nn(
            turned(prev_ref[:, vcols]), w_before.astype(BF)
        )
        o_ref[h] = mixture * (1.0 / total)
        l_ref[h] = jnp.broadcast_to(top + jnp.log(total) * LOG2E, (8, COLS))


def level_of(rows):
    r = rows.astype(F32)
    return r[0:1] + r[1:2] + r[2:3]


def joined(mixtures, levels):
    top = functools.reduce(jnp.maximum, levels)
    shares = [jnp.exp2(v - top) for v in levels]
    total = functools.reduce(jnp.add, shares)
    inverse = 1.0 / total
    mixture = functools.reduce(jnp.add, [m * (s * inverse) for m, s in zip(mixtures, shares)])
    return mixture, top + jnp.log(total) * LOG2E


def join_kernel(which, *refs):
    parts, o_ref = refs[:-1], refs[-1]
    for h in range(KVL):
        mixture, level = joined(
            [p[which, h, 0:HD, :].astype(F32) for p in parts], [level_of(p[which, h, HD:ROWS, :]) for p in parts]
        )
        o_ref[h, 0:HD, :] = mixture.astype(BF)
        o_ref[h, HD:ROWS, :] = packed_sum(level)


def last_kernel(a_ref, b_ref, c_ref, d_ref, e_ref, s_ref, l_ref, o_ref):
    parts = (a_ref, b_ref, c_ref, d_ref)
    for h in range(KVL):
        mixtures = [p[0, h, 0:HD, :].astype(F32) for p in parts] + [e_ref[h, 0:HD, :].astype(F32), s_ref[h]]
        levels = [level_of(p[0, h, HD:ROWS, :]) for p in parts] + [level_of(e_ref[h, HD:ROWS, :]), l_ref[h, 0:1, :]]
        mixture, _ = joined(mixtures, levels)
        for m in range(GROUP):
            c = (h * GROUP + m) * HD
            o_ref[:, c : c + HD] = mixture[:, m * BLOCK : (m + 1) * BLOCK].T.astype(BF)


def call(kernel, out_shape, smem=0, n=0, name=None):
    vm = pl.BlockSpec(memory_space=pltpu.VMEM)
    sm = pl.BlockSpec(memory_space=pltpu.SMEM)
    return pl.pallas_call(
        kernel,
        out_shape=out_shape,
        in_specs=[sm] * smem + [vm] * n,
        out_specs=jax.tree.map(lambda _: vm, out_shape),
        compiler_params=pltpu.CompilerParams(vmem_limit_bytes=48 << 20),
        name=name,
    )


def shards(queries, keys_new, values_new, cache_keys, cache_values, block_list, block_count, out_weight):
    ctx, head = lax.axis_index("ctx"), lax.axis_index("head")
    x, z = ctx // (NY * NZ), ctx % NZ
    core, half = head % CORES, head // CORES

    in_use = jnp.arange(block_list.shape[2])[None, :] < block_count
    listed = jnp.where(in_use, block_list[:, 0, :], -1).astype(BF).reshape(1, -1)
    listed = jnp.pad(listed, ((0, 7), (0, queries.shape[1] - listed.shape[1])))
    asked = jnp.concatenate([queries, listed], axis=0)
    asked_pair = jnp.stack([asked, send(asked, PAIRS_Y)])

    kv = call(pack_kernel, jax.ShapeDtypeStruct((KVL, CB_DEV, 2, BLOCK, HD), BF), n=2, name="pack")(
        cache_keys, cache_values
    )
    kvs = [kv] + [send(kv, pairs_along(-d, True)) for d in STEPS]
    asked_all = [asked_pair] + [send(asked_pair, pairs_along(-d, False)) for d in STEPS]

    prev = send(jnp.concatenate([keys_new, values_new], axis=1), PAIRS_PREV)
    local, local_level = call(
        stretch_kernel,
        (
            jax.ShapeDtypeStruct((KVL, HD, COLS), F32),
            jax.ShapeDtypeStruct((KVL, 8, COLS), F32),
        ),
        smem=1,
        n=4,
        name="stretch",
    )(jnp.minimum(ctx, 1).reshape(1), queries, keys_new, values_new, prev)

    steps = jnp.array((0,) + STEPS, jnp.int32)
    owners = jnp.where(core == 0, ctx - z + (z + steps) % NZ, ctx + ((x + steps) % NX - x) * NY * NZ)
    lists = jnp.stack([a[:, BLOCK, : KVL * block_list.shape[2]] for a in asked_all]).astype(jnp.int32)
    lists = lists.reshape(len(asked_all), NY, KVL, 1, block_list.shape[2])
    inside = lists // CB_DEV == owners[:, None]
    slot = lists % CB_DEV
    table = jnp.stack(
        [jnp.min(jnp.where(inside, slot, CB_DEV), axis=-1), jnp.max(jnp.where(inside, slot, -1), axis=-1)], axis=-1
    )
    table = jnp.clip(table, 0, CB_DEV - 1)

    attend = call(
        attend_kernel, jax.ShapeDtypeStruct((NY, KVL, ROWS, COLS), BF), smem=1, n=1 + len(kvs), name="attend"
    )
    parts = []
    for i in (3, 1, 2, 0):
        part = attend(table[i], asked_all[i], *kvs)
        parts.append(part if i == 0 else send(part, pairs_along(((0,) + STEPS)[i], False)))
    other = call(
        functools.partial(join_kernel, 1), jax.ShapeDtypeStruct((KVL, ROWS, COLS), BF), n=4, name="join"
    )(*parts)
    other = send(other, PAIRS_Y)
    attention = call(last_kernel, jax.ShapeDtypeStruct((BLOCK, KVL * COLS), BF), n=7, name="last")(
        *parts, other, local, local_level
    )

    width = out_weight.shape[1]
    product = jnp.dot(attention, out_weight, preferred_element_type=F32)
    product = product.reshape(HALVES, CORES, BLOCK // (HALVES * CORES), width)
    theirs = lax.dynamic_index_in_dim(product, 1 - core, 1, keepdims=False).astype(BF)
    mine = lax.dynamic_index_in_dim(product, core, 1, keepdims=False)
    chip = mine + send(theirs, PAIRS_CORE).astype(F32)
    theirs = lax.dynamic_index_in_dim(chip, 1 - half, 0, keepdims=False).astype(BF)
    mine = lax.dynamic_index_in_dim(chip, half, 0, keepdims=False)
    return (mine + send(theirs, PAIRS_LO).astype(F32)).astype(BF)


def solution(mesh):
    return jax.shard_map(
        shards,
        mesh=mesh,
        in_specs=(
            P("ctx", "head"),
            P("ctx", "head"),
            P("ctx", "head"),
            P("ctx", "head"),
            P("ctx", "head"),
            P("head", "ctx", None),
            P("head", "ctx"),
            P("head", None),
        ),
        out_specs=P(("ctx", "head"), None),
        check_vma=False,
    )
```

```python
import functools

import jax
import jax.numpy as jnp
from jax import lax
from jax.experimental import pallas as pl
from jax.experimental.pallas import tpu as pltpu
from jax.sharding import PartitionSpec as P

HD = 128
BLOCK = 128
CB_DEV = 8
KVL = 2
GROUP = 4
NX, NY, NZ = 4, 2, 4
HALVES, CORES = 2, 2
COLS = GROUP * BLOCK
ROWS = HD + 8
STEPS = (1, -1, 2)
SCALE = HD**-0.5
NEG = -1e30
AXES = ("ctx", "head")
COST = pl.CostEstimate(flops=1 << 31, transcendentals=1 << 20, bytes_accessed=12 << 20)
BF = jnp.bfloat16
F32 = jnp.float32


def flat(x, y, z, yl, c):
    return ((x * NY + y) * NZ + z) * (HALVES * CORES) + yl * CORES + c


def everyone():
    for x in range(NX):
        for y in range(NY):
            for z in range(NZ):
                for yl in range(HALVES):
                    for c in range(CORES):
                        yield x, y, z, yl, c


def moved(x, y, z, yl, c, by, keys):
    if (c == 0) == keys:
        return flat(x, y, (z + by) % NZ, yl, c)
    return flat((x + by) % NX, y, z, yl, c)


def pairs_along(by, keys):
    return [(flat(*d), moved(*d, by, keys)) for d in everyone()]


PAIRS_Y = [(flat(x, y, z, l, c), flat(x, 1 - y, z, l, c)) for x, y, z, l, c in everyone()]
PAIRS_CORE = [(flat(x, y, z, l, c), flat(x, y, z, l, 1 - c)) for x, y, z, l, c in everyone()]
PAIRS_LO = [(flat(x, y, z, l, c), flat(x, y, z, 1 - l, c)) for x, y, z, l, c in everyone()]
PAIRS_PREV = [
    (i * HALVES * CORES + h, (i + 1) * HALVES * CORES + h)
    for i in range(NX * NY * NZ - 1)
    for h in range(HALVES * CORES)
]


def send(array, pairs):
    return lax.ppermute(array, AXES, pairs)


def nt(a, b):
    return lax.dot_general(a, b, (((1,), (1,)), ((), ())), preferred_element_type=F32)


def nn(a, b):
    return lax.dot_general(a, b, (((1,), (0,)), ((), ())), preferred_element_type=F32)


def turned(block):
    return block.astype(F32).T.astype(BF)


def packed_sum(level):
    hi = level.astype(BF)
    rest = level - hi.astype(F32)
    mid = rest.astype(BF)
    low = (rest - mid.astype(F32)).astype(BF)
    return jnp.concatenate([hi.astype(F32), mid.astype(F32), low.astype(F32), jnp.zeros((5, COLS), F32)], axis=0).astype(BF)


def pack_kernel(list_ref, q_ref, k_ref, v_ref, asked_ref, kv_ref, v_buf, sems):
    rows = k_ref.shape[0]
    copies = [
        pltpu.make_async_copy(q_ref, asked_ref.at[0:BLOCK], sems.at[0]),
        pltpu.make_async_copy(v_ref, v_buf, sems.at[1]),
        pltpu.make_async_copy(k_ref, kv_ref.at[0:rows], sems.at[2]),
    ]
    for copy in copies:
        copy.start()
    asked_ref[BLOCK : BLOCK + 8, :] = jnp.zeros((8, asked_ref.shape[1]), BF)
    asked_ref[BLOCK : BLOCK + KVL, 0 : list_ref.shape[1]] = list_ref[...].astype(F32).astype(BF)
    copies[1].wait()
    for b in range(CB_DEV):
        for h in range(KVL):
            cols = slice(h * HD, (h + 1) * HD)
            kv_ref[rows + b * BLOCK : rows + (b + 1) * BLOCK, cols] = turned(v_buf[b * BLOCK : (b + 1) * BLOCK, cols])
    copies[0].wait()
    copies[2].wait()


def query_rows(q):
    return jnp.concatenate([q[:, m * HD : (m + 1) * HD] for m in range(GROUP)], axis=0)


def attend(tab_ref, q_ref, kvs, shard, y, h):
    q = query_rows(q_ref[y, 0:BLOCK, h * COLS : (h + 1) * COLS])
    cols = slice(h * HD, (h + 1) * HD)
    scores, offs, values = [], [], []
    for s, (keys, turned_values, base) in enumerate(kvs):
        first, second = tab_ref[y, h, shard + s, 0], tab_ref[y, h, shard + s, 1]
        for j, b in enumerate((first, second)):
            row = pl.multiple_of(b * BLOCK, BLOCK)
            scores.append(nt(keys[pl.ds(row, BLOCK), cols], q))
            values.append(turned_values[pl.ds(row + base, BLOCK), cols])
            offs.append(None if j == 0 else jnp.where(second == first, NEG, 0.0).astype(F32))
    tops = [
        jnp.max(t, axis=0, keepdims=True) if o is None else jnp.max(t, axis=0, keepdims=True) + o
        for t, o in zip(scores, offs)
    ]
    top = functools.reduce(jnp.maximum, tops) * SCALE
    weights = [jnp.exp(t * SCALE - (top if o is None else top - o)).astype(BF) for t, o in zip(scores, offs)]
    weights = jnp.concatenate(weights, axis=0)
    ones = jnp.ones((8, weights.shape[0]), BF)
    mixture = nn(jnp.concatenate([jnp.concatenate(values, axis=1), ones], axis=0), weights)
    return top, mixture[HD : HD + 1], mixture[0:HD]


def early_kernel(tab_ref, q0_ref, q1_ref, q2_ref, q3_ref, kv0_ref, kv1_ref, *out_refs):
    kvs = [(r, r, CB_DEV * BLOCK) for r in (kv0_ref, kv1_ref)]
    for i, q_ref in enumerate((q0_ref, q1_ref, q2_ref, q3_ref)):
        o_ref, s_ref = out_refs[2 * i : 2 * i + 2]
        for y in range(NY):
            for h in range(KVL):
                top, total, mixture = attend(tab_ref.at[i], q_ref, kvs, 0, y, h)
                o_ref[y, h] = mixture
                s_ref[y, h, 0:1, :] = top
                s_ref[y, h, 1:2, :] = total


def late_kernel(tab_ref, q_ref, kv2_ref, k3_ref, v3_ref, m_ref, s_ref, o_ref):
    kvs = [(kv2_ref, kv2_ref, CB_DEV * BLOCK), (k3_ref, v3_ref, 0)]
    for y in range(NY):
        for h in range(KVL):
            top, total, mixture = attend(tab_ref, q_ref, kvs, 2, y, h)
            top0, total0 = s_ref[y, h, 0:1, :], s_ref[y, h, 1:2, :]
            peak = jnp.maximum(top, top0)
            share, share0 = jnp.exp(top - peak), jnp.exp(top0 - peak)
            total = total * share + total0 * share0
            inverse = 1.0 / total
            o_ref[y, h, 0:HD, :] = (mixture * (share * inverse) + m_ref[y, h] * (share0 * inverse)).astype(BF)
            o_ref[y, h, HD:ROWS, :] = packed_sum(peak + jnp.log(total))


def stretch_kernel(first_ref, q_ref, k_ref, v_ref, prev_ref, o_ref, l_ref):
    off = jnp.where(first_ref[0] == 0, NEG, 0.0).astype(F32)
    key = lax.broadcasted_iota(jnp.int32, (BLOCK, COLS), 0)
    row = lax.broadcasted_iota(jnp.int32, (BLOCK, COLS), 1) % BLOCK
    for h in range(KVL):
        q = query_rows(q_ref[:, h * COLS : (h + 1) * COLS])
        cols = slice(h * HD, (h + 1) * HD)
        vcols = slice((KVL + h) * HD, (KVL + h + 1) * HD)
        own = jnp.where(key <= row, nt(k_ref[:, cols], q), NEG)
        before = nt(prev_ref[:, cols], q)
        top = jnp.maximum(
            jnp.max(own, axis=0, keepdims=True), jnp.max(before, axis=0, keepdims=True) + off
        ) * SCALE
        w_own = jnp.exp(own * SCALE - top)
        w_before = jnp.exp(before * SCALE - (top - off))
        total = jnp.sum(w_own, axis=0, keepdims=True) + jnp.sum(w_before, axis=0, keepdims=True)
        mixture = nn(turned(v_ref[:, cols]), w_own.astype(BF)) + nn(
            turned(prev_ref[:, vcols]), w_before.astype(BF)
        )
        o_ref[h] = mixture * (1.0 / total)
        l_ref[h] = jnp.broadcast_to(top + jnp.log(total), (8, COLS))


def level_of(rows):
    r = rows.astype(F32)
    return r[0:1] + r[1:2] + r[2:3]


def joined(mixtures, levels):
    top = functools.reduce(jnp.maximum, levels)
    shares = [jnp.exp(v - top) for v in levels]
    total = functools.reduce(jnp.add, shares)
    inverse = 1.0 / total
    mixture = functools.reduce(jnp.add, [m * (s * inverse) for m, s in zip(mixtures, shares)])
    return mixture, top + jnp.log(total)


def join_kernel(which, *refs):
    parts, o_ref = refs[:-1], refs[-1]
    for h in range(KVL):
        mixture, level = joined(
            [p[which, h, 0:HD, :].astype(F32) for p in parts], [level_of(p[which, h, HD:ROWS, :]) for p in parts]
        )
        o_ref[h, 0:HD, :] = mixture.astype(BF)
        o_ref[h, HD:ROWS, :] = packed_sum(level)


def last_kernel(
    place_ref, a_ref, b_ref, c_ref, d_ref, e_ref, s_ref, l_ref, w_ref, theirs_ref, mine_ref, att_ref, w_buf, sems
):
    chunks = sems.shape[0]
    width = w_buf.shape[1] // chunks
    copies = [
        pltpu.make_async_copy(
            w_ref.at[:, i * width : (i + 1) * width], w_buf.at[:, i * width : (i + 1) * width], sems.at[i]
        )
        for i in range(chunks)
    ]
    for copy in copies:
        copy.start()
    parts = (a_ref, b_ref, c_ref, d_ref)
    for h in range(KVL):
        mixtures = [p[0, h, 0:HD, :].astype(F32) for p in parts] + [e_ref[h, 0:HD, :].astype(F32), s_ref[h]]
        levels = [level_of(p[0, h, HD:ROWS, :]) for p in parts] + [level_of(e_ref[h, HD:ROWS, :]), l_ref[h, 0:1, :]]
        mixture, _ = joined(mixtures, levels)
        for m in range(GROUP):
            c = (h * GROUP + m) * HD
            att_ref[:, c : c + HD] = mixture[:, m * BLOCK : (m + 1) * BLOCK].T.astype(BF)
    half, core = place_ref[0], place_ref[1]
    share = BLOCK // (HALVES * CORES)
    order = [(1 - half, 1 - core), (half, 1 - core), (1 - half, core), (half, core)]
    rows = [att_ref[pl.ds(pl.multiple_of((a * CORES + b) * share, share), share), :] for a, b in order]
    rows = jnp.concatenate(rows, axis=0)
    for n in range(chunks):
        cols = slice(n * width, (n + 1) * width)
        copies[n].wait()
        product = nn(rows, w_buf[:, cols])
        for i in range(HALVES):
            theirs_ref[i, :, cols] = product[i * share : (i + 1) * share].astype(BF)
            mine_ref[i, :, cols] = product[(HALVES + i) * share : (HALVES + i + 1) * share]


def call(kernel, out_shape, smem=0, n=0, hbm=0, name=None, memory=24, scratch=(), cost=None):
    spaces = [pltpu.SMEM] * smem + [pltpu.VMEM] * n + [pltpu.HBM] * hbm
    vm = pl.BlockSpec(memory_space=pltpu.VMEM)
    return pl.pallas_call(
        kernel,
        out_shape=out_shape,
        in_specs=[pl.BlockSpec(memory_space=space) for space in spaces],
        out_specs=jax.tree.map(lambda _: vm, out_shape),
        scratch_shapes=scratch,
        compiler_params=pltpu.CompilerParams(vmem_limit_bytes=memory << 20),
        cost_estimate=cost,
        name=name,
    )


def shape(dims, dtype):
    return jax.ShapeDtypeStruct(dims, dtype)


def shards(queries, keys_new, values_new, cache_keys, cache_values, block_list, block_count, out_weight):
    ctx, head = lax.axis_index("ctx"), lax.axis_index("head")
    x, z = ctx // (NY * NZ), ctx % NZ
    core, half = head % CORES, head // CORES
    sel = block_list.shape[2]

    rows = cache_keys.shape[0]
    asked, kv = call(
        pack_kernel,
        (shape((queries.shape[0] + 8, queries.shape[1]), BF), shape((2 * rows, cache_keys.shape[1]), BF)),
        n=1,
        hbm=3,
        name="pack",
        scratch=[pltpu.VMEM(cache_values.shape, BF), pltpu.SemaphoreType.DMA((3,))],
    )(block_list.reshape(KVL, sel), *(pltpu.with_memory_space_constraint(a, pltpu.HBM) for a in (queries, cache_keys, cache_values)))
    asked_pair = jnp.stack([asked, send(asked, PAIRS_Y)])
    after, before = send(kv, pairs_along(-1, True)), send(kv, pairs_along(1, True))
    asked_all = [asked_pair] + [send(asked_pair, pairs_along(-d, False)) for d in STEPS]
    half_keys, half_values = after[:rows], before[rows:]
    asked_all, half_keys, half_values = lax.optimization_barrier((asked_all, half_keys, half_values))
    far_keys = send(half_keys, pairs_along(-1, True))
    far_values = send(half_values, pairs_along(1, True))

    steps = jnp.array((0,) + STEPS, jnp.int32)
    owners = jnp.where(core == 0, ctx - z + (z + steps) % NZ, ctx + ((x + steps) % NX - x) * NY * NZ)
    lists = jnp.stack([a[:, BLOCK : BLOCK + KVL, None, :sel] for a in asked_all]).astype(jnp.int32)
    inside = lists // CB_DEV == owners[:, None]
    slot = lists % CB_DEV
    table = jnp.stack(
        [jnp.min(jnp.where(inside, slot, CB_DEV), axis=-1), jnp.max(jnp.where(inside, slot, -1), axis=-1)], axis=-1
    )
    table = jnp.clip(table, 0, CB_DEV - 1)
    begun = call(
        early_kernel,
        (shape((NY, KVL, HD, COLS), F32), shape((NY, KVL, 8, COLS), F32)) * 4,
        smem=1,
        n=6,
        name="early",
        cost=COST,
    )(table, *asked_all, kv, after)
    begun, keys_new, values_new = lax.optimization_barrier((begun, keys_new, values_new))

    prev = send(jnp.concatenate([keys_new, values_new], axis=1), PAIRS_PREV)
    local = call(
        stretch_kernel, (shape((KVL, HD, COLS), F32), shape((KVL, 8, COLS), F32)), smem=1, n=4, name="stretch"
    )(jnp.minimum(ctx, 1).reshape(1), queries, keys_new, values_new, prev)

    parts = []
    for i in (3, 1, 2, 0):
        part = call(late_kernel, shape((NY, KVL, ROWS, COLS), BF), smem=1, n=6, name="late", cost=COST)(
            table[i], asked_all[i], before, far_keys, far_values, begun[2 * i], begun[2 * i + 1]
        )
        parts.append(part if i == 0 else send(part, pairs_along(((0,) + STEPS)[i], False)))
    other = call(functools.partial(join_kernel, 1), shape((KVL, ROWS, COLS), BF), n=4, name="join")(*parts)
    other = send(other, PAIRS_Y)

    share, width = BLOCK // (HALVES * CORES), out_weight.shape[1]
    theirs, mine = call(
        last_kernel,
        (shape((HALVES, share, width), BF), shape((HALVES, share, width), F32)),
        smem=1,
        n=7,
        hbm=1,
        name="last",
        scratch=[
            pltpu.VMEM((BLOCK, KVL * COLS), BF),
            pltpu.VMEM(out_weight.shape, BF),
            pltpu.SemaphoreType.DMA((4,)),
        ],
    )(jnp.stack([half, core]), *parts, other, *local, pltpu.with_memory_space_constraint(out_weight, pltpu.HBM))
    chip = mine + send(theirs, PAIRS_CORE).astype(F32)
    return (chip[1] + send(chip[0].astype(BF), PAIRS_LO).astype(F32)).astype(BF)


def solution(mesh):
    return jax.shard_map(
        shards,
        mesh=mesh,
        in_specs=(
            P("ctx", "head"),
            P("ctx", "head"),
            P("ctx", "head"),
            P("ctx", "head"),
            P("ctx", "head"),
            P("head", "ctx", None),
            P("head", "ctx"),
            P("head", None),
        ),
        out_specs=P(("ctx", "head"), None),
        check_vma=False,
    )
```

```python
import functools

import jax
import jax.numpy as jnp
from jax import lax
from jax.experimental import pallas as pl
from jax.experimental.pallas import tpu as pltpu
from jax.sharding import PartitionSpec as P

HD = 128
BLOCK = 128
CB_DEV = 8
KVL = 2
GROUP = 4
NX, NY, NZ = 4, 2, 4
HALVES, CORES = 2, 2
COLS = GROUP * BLOCK
ROWS = HD + 8
STEPS = (1, -1, 2)
SCALE = HD**-0.5
NEG = -1e30
AXES = ("ctx", "head")
COST = pl.CostEstimate(flops=1 << 31, transcendentals=1 << 20, bytes_accessed=12 << 20)
BF = jnp.bfloat16
F32 = jnp.float32


def flat(x, y, z, yl, c):
    return ((x * NY + y) * NZ + z) * (HALVES * CORES) + yl * CORES + c


def everyone():
    for x in range(NX):
        for y in range(NY):
            for z in range(NZ):
                for yl in range(HALVES):
                    for c in range(CORES):
                        yield x, y, z, yl, c


def moved(x, y, z, yl, c, by, keys):
    if (c == 0) == keys:
        return flat(x, y, (z + by) % NZ, yl, c)
    return flat((x + by) % NX, y, z, yl, c)


def pairs_along(by, keys):
    return [(flat(*d), moved(*d, by, keys)) for d in everyone()]


PAIRS_Y = [(flat(x, y, z, l, c), flat(x, 1 - y, z, l, c)) for x, y, z, l, c in everyone()]
PAIRS_CORE = [(flat(x, y, z, l, c), flat(x, y, z, l, 1 - c)) for x, y, z, l, c in everyone()]
PAIRS_LO = [(flat(x, y, z, l, c), flat(x, y, z, 1 - l, c)) for x, y, z, l, c in everyone()]
PAIRS_PREV = [
    (i * HALVES * CORES + h, (i + 1) * HALVES * CORES + h)
    for i in range(NX * NY * NZ - 1)
    for h in range(HALVES * CORES)
]


def send(array, pairs):
    return lax.ppermute(array, AXES, pairs)


def nt(a, b):
    return lax.dot_general(a, b, (((1,), (1,)), ((), ())), preferred_element_type=F32)


def nn(a, b):
    return lax.dot_general(a, b, (((1,), (0,)), ((), ())), preferred_element_type=F32)


def turned(block):
    return block.astype(F32).T.astype(BF)


def packed_sum(level):
    hi = level.astype(BF)
    rest = level - hi.astype(F32)
    mid = rest.astype(BF)
    low = (rest - mid.astype(F32)).astype(BF)
    return jnp.concatenate([hi.astype(F32), mid.astype(F32), low.astype(F32), jnp.zeros((5, COLS), F32)], axis=0).astype(BF)


def pack_kernel(list_ref, q_ref, k_ref, v_ref, asked_ref, kv_ref, v_buf, sems):
    rows = k_ref.shape[0]
    copies = [
        pltpu.make_async_copy(q_ref, asked_ref.at[0:BLOCK], sems.at[0]),
        pltpu.make_async_copy(v_ref, v_buf, sems.at[1]),
        pltpu.make_async_copy(k_ref, kv_ref.at[0:rows], sems.at[2]),
    ]
    for copy in copies:
        copy.start()
    asked_ref[BLOCK : BLOCK + 8, :] = jnp.zeros((8, asked_ref.shape[1]), BF)
    asked_ref[BLOCK : BLOCK + KVL, 0 : list_ref.shape[1]] = list_ref[...].astype(F32).astype(BF)
    copies[1].wait()
    for b in range(CB_DEV):
        for h in range(KVL):
            cols = slice(h * HD, (h + 1) * HD)
            kv_ref[rows + b * BLOCK : rows + (b + 1) * BLOCK, cols] = turned(v_buf[b * BLOCK : (b + 1) * BLOCK, cols])
    copies[0].wait()
    copies[2].wait()


def query_rows(q):
    return jnp.concatenate([q[:, m * HD : (m + 1) * HD] for m in range(GROUP)], axis=0)


def attend(tab_ref, q_ref, kvs, shard, y, h):
    q = query_rows(q_ref[y, 0:BLOCK, h * COLS : (h + 1) * COLS])
    cols = slice(h * HD, (h + 1) * HD)
    scores, offs, values = [], [], []
    for s, (keys, turned_values, base) in enumerate(kvs):
        first, second = tab_ref[y, h, shard + s, 0], tab_ref[y, h, shard + s, 1]
        for j, b in enumerate((first, second)):
            row = pl.multiple_of(b * BLOCK, BLOCK)
            scores.append(nt(keys[pl.ds(row, BLOCK), cols], q))
            values.append(turned_values[pl.ds(row + base, BLOCK), cols])
            offs.append(None if j == 0 else jnp.where(second == first, NEG, 0.0).astype(F32))
    tops = [
        jnp.max(t, axis=0, keepdims=True) if o is None else jnp.max(t, axis=0, keepdims=True) + o
        for t, o in zip(scores, offs)
    ]
    top = functools.reduce(jnp.maximum, tops) * SCALE
    weights = [jnp.exp(t * SCALE - (top if o is None else top - o)).astype(BF) for t, o in zip(scores, offs)]
    weights = jnp.concatenate(weights, axis=0)
    ones = jnp.ones((8, weights.shape[0]), BF)
    mixture = nn(jnp.concatenate([jnp.concatenate(values, axis=1), ones], axis=0), weights)
    return top, mixture[HD : HD + 1], mixture[0:HD]


def early_kernel(count, tab_ref, turn_ref, kv0_ref, kv1_ref, kv2_ref, *refs):
    kvs = [(r, r, CB_DEV * BLOCK) for r in (kv0_ref, kv1_ref, kv2_ref)]
    refs[-1][...] = turn_ref[...]
    for i, q_ref in enumerate(refs[:count]):
        o_ref, s_ref = refs[count + 2 * i : count + 2 * i + 2]
        for y in range(NY):
            for h in range(KVL):
                top, total, mixture = attend(tab_ref.at[i], q_ref, kvs, 0, y, h)
                o_ref[y, h] = mixture
                s_ref[y, h, 0:1, :] = top
                s_ref[y, h, 1:2, :] = total


def late_kernel(count, tab_ref, k3_ref, v3_ref, *refs):
    kvs = [(k3_ref, v3_ref, 0)]
    inputs, outputs = refs[: 3 * count], refs[3 * count :]
    for i, o_ref in enumerate(outputs):
        q_ref, m_ref, s_ref = inputs[3 * i : 3 * i + 3]
        for y in range(NY):
            for h in range(KVL):
                top, total, mixture = attend(tab_ref.at[i], q_ref, kvs, 3, y, h)
                top0, total0 = s_ref[y, h, 0:1, :], s_ref[y, h, 1:2, :]
                peak = jnp.maximum(top, top0)
                share, share0 = jnp.exp(top - peak), jnp.exp(top0 - peak)
                total = total * share + total0 * share0
                inverse = 1.0 / total
                o_ref[y, h, 0:HD, :] = (mixture * (share * inverse) + m_ref[y, h] * (share0 * inverse)).astype(BF)
                o_ref[y, h, HD:ROWS, :] = packed_sum(peak + jnp.log(total))


def stretch_kernel(first_ref, q_ref, k_ref, v_ref, prev_ref, o_ref, l_ref):
    off = jnp.where(first_ref[0] == 0, NEG, 0.0).astype(F32)
    key = lax.broadcasted_iota(jnp.int32, (BLOCK, COLS), 0)
    row = lax.broadcasted_iota(jnp.int32, (BLOCK, COLS), 1) % BLOCK
    for h in range(KVL):
        q = query_rows(q_ref[:, h * COLS : (h + 1) * COLS])
        cols = slice(h * HD, (h + 1) * HD)
        vcols = slice((KVL + h) * HD, (KVL + h + 1) * HD)
        own = jnp.where(key <= row, nt(k_ref[:, cols], q), NEG)
        before = nt(prev_ref[:, cols], q)
        top = jnp.maximum(
            jnp.max(own, axis=0, keepdims=True), jnp.max(before, axis=0, keepdims=True) + off
        ) * SCALE
        w_own = jnp.exp(own * SCALE - top)
        w_before = jnp.exp(before * SCALE - (top - off))
        total = jnp.sum(w_own, axis=0, keepdims=True) + jnp.sum(w_before, axis=0, keepdims=True)
        mixture = nn(turned(v_ref[:, cols]), w_own.astype(BF)) + nn(
            turned(prev_ref[:, vcols]), w_before.astype(BF)
        )
        o_ref[h] = mixture * (1.0 / total)
        l_ref[h] = jnp.broadcast_to(top + jnp.log(total), (8, COLS))


def level_of(rows):
    r = rows.astype(F32)
    return r[0:1] + r[1:2] + r[2:3]


def joined(mixtures, levels):
    top = functools.reduce(jnp.maximum, levels)
    shares = [jnp.exp(v - top) for v in levels]
    total = functools.reduce(jnp.add, shares)
    inverse = 1.0 / total
    mixture = functools.reduce(jnp.add, [m * (s * inverse) for m, s in zip(mixtures, shares)])
    return mixture, top + jnp.log(total)


def join_kernel(which, *refs):
    parts, o_ref = refs[:-1], refs[-1]
    for h in range(KVL):
        mixture, level = joined(
            [p[which, h, 0:HD, :].astype(F32) for p in parts], [level_of(p[which, h, HD:ROWS, :]) for p in parts]
        )
        o_ref[h, 0:HD, :] = mixture.astype(BF)
        o_ref[h, HD:ROWS, :] = packed_sum(level)


def home_kernel(a_ref, b_ref, c_ref, d_ref, s_ref, l_ref, w_ref, o_ref, v_ref, copy_ref, sem):
    copy = pltpu.make_async_copy(w_ref, copy_ref, sem)
    copy.start()
    parts = (a_ref, b_ref, c_ref, d_ref)
    for h in range(KVL):
        mixtures = [p[0, h, 0:HD, :].astype(F32) for p in parts] + [s_ref[h]]
        levels = [level_of(p[0, h, HD:ROWS, :]) for p in parts] + [l_ref[h, 0:1, :]]
        mixture, level = joined(mixtures, levels)
        o_ref[h] = mixture
        v_ref[h] = jnp.broadcast_to(level, (8, COLS))
    copy.wait()


def last_kernel(place_ref, m_ref, v_ref, e_ref, w_ref, theirs_ref, mine_ref, att_ref):
    for h in range(KVL):
        mixture, _ = joined(
            [m_ref[h], e_ref[h, 0:HD, :].astype(F32)], [v_ref[h, 0:1, :], level_of(e_ref[h, HD:ROWS, :])]
        )
        for m in range(GROUP):
            c = (h * GROUP + m) * HD
            att_ref[:, c : c + HD] = mixture[:, m * BLOCK : (m + 1) * BLOCK].T.astype(BF)
    half, core = place_ref[0], place_ref[1]
    share = BLOCK // (HALVES * CORES)
    order = [(1 - half, 1 - core), (half, 1 - core), (1 - half, core), (half, core)]
    rows = [att_ref[pl.ds(pl.multiple_of((a * CORES + b) * share, share), share), :] for a, b in order]
    rows = jnp.concatenate(rows, axis=0)
    for n in range(4):
        cols = slice(n * w_ref.shape[1] // 4, (n + 1) * w_ref.shape[1] // 4)
        product = nn(rows, w_ref[:, cols])
        for i in range(HALVES):
            theirs_ref[i, :, cols] = product[i * share : (i + 1) * share].astype(BF)
            mine_ref[i, :, cols] = product[(HALVES + i) * share : (HALVES + i + 1) * share]


def call(kernel, out_shape, smem=0, n=0, hbm=0, name=None, memory=24, scratch=(), cost=None):
    spaces = [pltpu.SMEM] * smem + [pltpu.VMEM] * n + [pltpu.HBM] * hbm
    vm = pl.BlockSpec(memory_space=pltpu.VMEM)
    return pl.pallas_call(
        kernel,
        out_shape=out_shape,
        in_specs=[pl.BlockSpec(memory_space=space) for space in spaces],
        out_specs=jax.tree.map(lambda _: vm, out_shape),
        scratch_shapes=scratch,
        compiler_params=pltpu.CompilerParams(vmem_limit_bytes=memory << 20),
        cost_estimate=cost,
        name=name,
    )


def shape(dims, dtype):
    return jax.ShapeDtypeStruct(dims, dtype)


def shards(queries, keys_new, values_new, cache_keys, cache_values, block_list, block_count, out_weight):
    ctx, head = lax.axis_index("ctx"), lax.axis_index("head")
    x, z = ctx // (NY * NZ), ctx % NZ
    core, half = head % CORES, head // CORES
    sel = block_list.shape[2]

    rows = cache_keys.shape[0]
    asked, kv = call(
        pack_kernel,
        (shape((queries.shape[0] + 8, queries.shape[1]), BF), shape((2 * rows, cache_keys.shape[1]), BF)),
        n=1,
        hbm=3,
        name="pack",
        scratch=[pltpu.VMEM(cache_values.shape, BF), pltpu.SemaphoreType.DMA((3,))],
    )(block_list.reshape(KVL, sel), *(pltpu.with_memory_space_constraint(a, pltpu.HBM) for a in (queries, cache_keys, cache_values)))
    asked_pair = jnp.stack([asked, send(asked, PAIRS_Y)])
    after, before = send(kv, pairs_along(-1, True)), send(kv, pairs_along(1, True))
    asked_all = [asked_pair] + [send(asked_pair, pairs_along(-d, False)) for d in STEPS]
    half_keys, half_values = after[:rows], before[rows:]
    asked_pair, half_keys, half_values = lax.optimization_barrier((asked_pair, half_keys, half_values))
    far_keys = send(half_keys, pairs_along(-1, True))
    far_values = send(half_values, pairs_along(1, True))

    steps = jnp.array((0,) + STEPS, jnp.int32)
    owners = jnp.where(core == 0, ctx - z + (z + steps) % NZ, ctx + ((x + steps) % NX - x) * NY * NZ)

    def begin(asked, turn):
        lists = jnp.stack([a[:, BLOCK : BLOCK + KVL, None, :sel] for a in asked]).astype(jnp.int32)
        inside = lists // CB_DEV == owners[:, None]
        slot = lists % CB_DEV
        table = jnp.stack(
            [jnp.min(jnp.where(inside, slot, CB_DEV), axis=-1), jnp.max(jnp.where(inside, slot, -1), axis=-1)], axis=-1
        )
        table = jnp.clip(table, 0, CB_DEV - 1)
        n = len(asked)
        *begun, turn = call(
            functools.partial(early_kernel, n),
            (shape((NY, KVL, HD, COLS), F32), shape((NY, KVL, 8, COLS), F32)) * n + (shape((8, HD), F32),),
            smem=1,
            n=4 + n,
            name="early",
            cost=pl.CostEstimate(flops=0, transcendentals=0, bytes_accessed=1024),
        )(table, turn, kv, after, before, *asked)
        return [(table[i], asked[i], *begun[2 * i : 2 * i + 2]) for i in range(n)], turn

    begun, turn = begin([asked_pair], jnp.zeros((8, HD), F32))
    rest, turn = lax.optimization_barrier((asked_all[1:], turn))
    ended, turn = begin(rest, turn)
    begun = begun + ended

    parts = []
    for group in ((3,), (1,), (2, 0)):
        inputs = [a for i in group for a in begun[i][1:]]
        partials = call(
            functools.partial(late_kernel, len(group)),
            (shape((NY, KVL, ROWS, COLS), BF),) * len(group),
            smem=1,
            n=2 + len(inputs),
            name="late",
            cost=COST,
        )(jnp.stack([begun[i][0] for i in group]), far_keys, far_values, *inputs)
        parts += [p if i == 0 else send(p, pairs_along(((0,) + STEPS)[i], False)) for i, p in zip(group, partials)]
    stretch_rows = jnp.concatenate([keys_new, values_new], axis=1)
    prev = send(stretch_rows, PAIRS_PREV)
    other = call(functools.partial(join_kernel, 1), shape((KVL, ROWS, COLS), BF), n=4, name="join")(*parts)
    other, prev = lax.optimization_barrier((other, prev))
    local = call(
        stretch_kernel, (shape((KVL, HD, COLS), F32), shape((KVL, 8, COLS), F32)), smem=1, n=4, name="stretch"
    )(jnp.minimum(ctx, 1).reshape(1), queries, keys_new, values_new, prev)
    other = send(other, PAIRS_Y)
    *home, weight = call(
        home_kernel,
        (
            shape((KVL, HD, COLS), F32),
            shape((KVL, 8, COLS), F32),
            shape(out_weight.shape, BF),
        ),
        n=6,
        hbm=1,
        name="home",
        scratch=[pltpu.SemaphoreType.DMA],
        memory=16,
        cost=COST,
    )(*parts, *local, pltpu.with_memory_space_constraint(out_weight, pltpu.HBM))

    share, width = BLOCK // (HALVES * CORES), out_weight.shape[1]
    theirs, mine = call(
        last_kernel,
        (shape((HALVES, share, width), BF), shape((HALVES, share, width), F32)),
        smem=1,
        n=4,
        name="last",
        scratch=[pltpu.VMEM((BLOCK, KVL * COLS), BF)],
        memory=16,
    )(jnp.stack([half, core]), *home, other, weight)
    chip = mine + send(theirs, PAIRS_CORE).astype(F32)
    return (chip[1] + send(chip[0].astype(BF), PAIRS_LO).astype(F32)).astype(BF)


def solution(mesh):
    return jax.shard_map(
        shards,
        mesh=mesh,
        in_specs=(
            P("ctx", "head"),
            P("ctx", "head"),
            P("ctx", "head"),
            P("ctx", "head"),
            P("ctx", "head"),
            P("head", "ctx", None),
            P("head", "ctx"),
            P("head", None),
        ),
        out_specs=P(("ctx", "head"), None),
        check_vma=False,
    )
```

```python
import functools

import jax
import jax.numpy as jnp
from jax import lax
from jax.experimental import pallas as pl
from jax.experimental.pallas import tpu as pltpu
from jax.sharding import PartitionSpec as P

HD = 128
BLOCK = 128
CB_DEV = 8
KVL = 2
GROUP = 4
NX, NY, NZ = 4, 2, 4
HALVES, CORES = 2, 2
COLS = GROUP * BLOCK
ROWS = HD + 8
STEPS = (1, -1, 2)
SCALE = HD**-0.5
NEG = -1e30
AXES = ("ctx", "head")
COST = pl.CostEstimate(flops=1 << 31, transcendentals=1 << 20, bytes_accessed=12 << 20)
BF = jnp.bfloat16
F32 = jnp.float32


def flat(x, y, z, yl, c):
    return ((x * NY + y) * NZ + z) * (HALVES * CORES) + yl * CORES + c


def everyone():
    for x in range(NX):
        for y in range(NY):
            for z in range(NZ):
                for yl in range(HALVES):
                    for c in range(CORES):
                        yield x, y, z, yl, c


def moved(x, y, z, yl, c, by, keys):
    if (c == 0) == keys:
        return flat(x, y, (z + by) % NZ, yl, c)
    return flat((x + by) % NX, y, z, yl, c)


def pairs_along(by, keys):
    return [(flat(*d), moved(*d, by, keys)) for d in everyone()]


PAIRS_Y = [(flat(x, y, z, l, c), flat(x, 1 - y, z, l, c)) for x, y, z, l, c in everyone()]
PAIRS_CORE = [(flat(x, y, z, l, c), flat(x, y, z, l, 1 - c)) for x, y, z, l, c in everyone()]
PAIRS_LO = [(flat(x, y, z, l, c), flat(x, y, z, 1 - l, c)) for x, y, z, l, c in everyone()]
PAIRS_PREV = [
    (i * HALVES * CORES + h, (i + 1) * HALVES * CORES + h)
    for i in range(NX * NY * NZ - 1)
    for h in range(HALVES * CORES)
]


def send(array, pairs):
    return lax.ppermute(array, AXES, pairs)


def nt(a, b):
    return lax.dot_general(a, b, (((1,), (1,)), ((), ())), preferred_element_type=F32)


def nn(a, b):
    return lax.dot_general(a, b, (((1,), (0,)), ((), ())), preferred_element_type=F32)


def turned(block):
    return block.astype(F32).T.astype(BF)


def packed_sum(level):
    hi = level.astype(BF)
    rest = level - hi.astype(F32)
    mid = rest.astype(BF)
    low = (rest - mid.astype(F32)).astype(BF)
    return jnp.concatenate([hi.astype(F32), mid.astype(F32), low.astype(F32), jnp.zeros((5, COLS), F32)], axis=0).astype(BF)


def pack_kernel(list_ref, q_ref, k_ref, v_ref, asked_ref, kv_ref, v_buf, list_buf, sems):
    rows = k_ref.shape[0]
    copies = [
        pltpu.make_async_copy(q_ref, asked_ref.at[0:BLOCK], sems.at[0]),
        pltpu.make_async_copy(v_ref, v_buf, sems.at[1]),
        pltpu.make_async_copy(k_ref, kv_ref.at[0:rows], sems.at[2]),
        pltpu.make_async_copy(list_ref, list_buf, sems.at[3]),
    ]
    for copy in copies:
        copy.start()
    asked_ref[BLOCK : BLOCK + 8, :] = jnp.zeros((8, asked_ref.shape[1]), BF)
    copies[3].wait()
    for h in range(KVL):
        asked_ref[BLOCK + h : BLOCK + h + 1, 0 : list_ref.shape[2]] = list_buf[h].astype(F32).astype(BF)
    copies[1].wait()
    for b in range(CB_DEV):
        for h in range(KVL):
            cols = slice(h * HD, (h + 1) * HD)
            kv_ref[rows + b * BLOCK : rows + (b + 1) * BLOCK, cols] = turned(v_buf[b * BLOCK : (b + 1) * BLOCK, cols])
    copies[0].wait()
    copies[2].wait()


def query_rows(q):
    return jnp.concatenate([q[:, m * HD : (m + 1) * HD] for m in range(GROUP)], axis=0)


def attend(tab_ref, q_ref, kvs, shard, y, h):
    q = query_rows(q_ref[y, 0:BLOCK, h * COLS : (h + 1) * COLS])
    cols = slice(h * HD, (h + 1) * HD)
    scores, offs, values = [], [], []
    for s, (keys, turned_values, base) in enumerate(kvs):
        first, second = tab_ref[y, h, shard + s, 0], tab_ref[y, h, shard + s, 1]
        for j, b in enumerate((first, second)):
            row = pl.multiple_of(b * BLOCK, BLOCK)
            scores.append(nt(keys[pl.ds(row, BLOCK), cols], q))
            values.append(turned_values[pl.ds(row + base, BLOCK), cols])
            offs.append(None if j == 0 else jnp.where(second == first, NEG, 0.0).astype(F32))
    tops = [
        jnp.max(t, axis=0, keepdims=True) if o is None else jnp.max(t, axis=0, keepdims=True) + o
        for t, o in zip(scores, offs)
    ]
    top = functools.reduce(jnp.maximum, tops) * SCALE
    weights = [jnp.exp(t * SCALE - (top if o is None else top - o)).astype(BF) for t, o in zip(scores, offs)]
    weights = jnp.concatenate(weights, axis=0)
    ones = jnp.ones((8, weights.shape[0]), BF)
    mixture = nn(jnp.concatenate([jnp.concatenate(values, axis=1), ones], axis=0), weights)
    return top, mixture[HD : HD + 1], mixture[0:HD]


def early_kernel(count, tab_ref, turn_ref, kv0_ref, kv1_ref, kv2_ref, *refs):
    kvs = [(r, r, CB_DEV * BLOCK) for r in (kv0_ref, kv1_ref, kv2_ref)]
    refs[-1][...] = turn_ref[...]
    for i, q_ref in enumerate(refs[:count]):
        o_ref, s_ref = refs[count + 2 * i : count + 2 * i + 2]
        for y in range(NY):
            for h in range(KVL):
                top, total, mixture = attend(tab_ref.at[i], q_ref, kvs, 0, y, h)
                o_ref[y, h] = mixture
                s_ref[y, h, 0:1, :] = top
                s_ref[y, h, 1:2, :] = total


def late_kernel(count, tab_ref, k3_ref, v3_ref, *refs):
    kvs = [(k3_ref, v3_ref, 0)]
    inputs, outputs = refs[: 3 * count], refs[3 * count :]
    for i, o_ref in enumerate(outputs):
        q_ref, m_ref, s_ref = inputs[3 * i : 3 * i + 3]
        for y in range(NY):
            for h in range(KVL):
                top, total, mixture = attend(tab_ref.at[i], q_ref, kvs, 3, y, h)
                top0, total0 = s_ref[y, h, 0:1, :], s_ref[y, h, 1:2, :]
                peak = jnp.maximum(top, top0)
                share, share0 = jnp.exp(top - peak), jnp.exp(top0 - peak)
                total = total * share + total0 * share0
                inverse = 1.0 / total
                o_ref[y, h, 0:HD, :] = (mixture * (share * inverse) + m_ref[y, h] * (share0 * inverse)).astype(BF)
                o_ref[y, h, HD:ROWS, :] = packed_sum(peak + jnp.log(total))


def stretch_kernel(first_ref, q_ref, k_ref, v_ref, prev_ref, o_ref, l_ref):
    off = jnp.where(first_ref[0] == 0, NEG, 0.0).astype(F32)
    key = lax.broadcasted_iota(jnp.int32, (BLOCK, COLS), 0)
    row = lax.broadcasted_iota(jnp.int32, (BLOCK, COLS), 1) % BLOCK
    for h in range(KVL):
        q = query_rows(q_ref[:, h * COLS : (h + 1) * COLS])
        cols = slice(h * HD, (h + 1) * HD)
        vcols = slice((KVL + h) * HD, (KVL + h + 1) * HD)
        own = jnp.where(key <= row, nt(k_ref[:, cols], q), NEG)
        before = nt(prev_ref[:, cols], q)
        top = jnp.maximum(
            jnp.max(own, axis=0, keepdims=True), jnp.max(before, axis=0, keepdims=True) + off
        ) * SCALE
        w_own = jnp.exp(own * SCALE - top)
        w_before = jnp.exp(before * SCALE - (top - off))
        total = jnp.sum(w_own, axis=0, keepdims=True) + jnp.sum(w_before, axis=0, keepdims=True)
        mixture = nn(turned(v_ref[:, cols]), w_own.astype(BF)) + nn(
            turned(prev_ref[:, vcols]), w_before.astype(BF)
        )
        o_ref[h] = mixture * (1.0 / total)
        l_ref[h] = jnp.broadcast_to(top + jnp.log(total), (8, COLS))


def level_of(rows):
    r = rows.astype(F32)
    return r[0:1] + r[1:2] + r[2:3]


def joined(mixtures, levels):
    top = functools.reduce(jnp.maximum, levels)
    shares = [jnp.exp(v - top) for v in levels]
    total = functools.reduce(jnp.add, shares)
    inverse = 1.0 / total
    mixture = functools.reduce(jnp.add, [m * (s * inverse) for m, s in zip(mixtures, shares)])
    return mixture, top + jnp.log(total)


def join_kernel(which, *refs):
    parts, o_ref = refs[:-1], refs[-1]
    for h in range(KVL):
        mixture, level = joined(
            [p[which, h, 0:HD, :].astype(F32) for p in parts], [level_of(p[which, h, HD:ROWS, :]) for p in parts]
        )
        o_ref[h, 0:HD, :] = mixture.astype(BF)
        o_ref[h, HD:ROWS, :] = packed_sum(level)


def home_kernel(a_ref, b_ref, c_ref, d_ref, s_ref, l_ref, w_ref, o_ref, v_ref, copy_ref, sem):
    copy = pltpu.make_async_copy(w_ref, copy_ref, sem)
    copy.start()
    parts = (a_ref, b_ref, c_ref, d_ref)
    for h in range(KVL):
        mixtures = [p[0, h, 0:HD, :].astype(F32) for p in parts] + [s_ref[h]]
        levels = [level_of(p[0, h, HD:ROWS, :]) for p in parts] + [l_ref[h, 0:1, :]]
        mixture, level = joined(mixtures, levels)
        o_ref[h] = mixture
        v_ref[h] = jnp.broadcast_to(level, (8, COLS))
    copy.wait()


def last_kernel(place_ref, m_ref, v_ref, e_ref, w_ref, theirs_ref, mine_ref, att_ref):
    for h in range(KVL):
        mixture, _ = joined(
            [m_ref[h], e_ref[h, 0:HD, :].astype(F32)], [v_ref[h, 0:1, :], level_of(e_ref[h, HD:ROWS, :])]
        )
        for m in range(GROUP):
            c = (h * GROUP + m) * HD
            att_ref[:, c : c + HD] = mixture[:, m * BLOCK : (m + 1) * BLOCK].T.astype(BF)
    half, core = place_ref[0], place_ref[1]
    share = BLOCK // (HALVES * CORES)
    order = [(1 - half, 1 - core), (half, 1 - core), (1 - half, core), (half, core)]
    rows = [att_ref[pl.ds(pl.multiple_of((a * CORES + b) * share, share), share), :] for a, b in order]
    rows = jnp.concatenate(rows, axis=0)
    for n in range(4):
        cols = slice(n * w_ref.shape[1] // 4, (n + 1) * w_ref.shape[1] // 4)
        product = nn(rows, w_ref[:, cols])
        for i in range(HALVES):
            theirs_ref[i, :, cols] = product[i * share : (i + 1) * share].astype(BF)
            mine_ref[i, :, cols] = product[(HALVES + i) * share : (HALVES + i + 1) * share]


def call(kernel, out_shape, smem=0, n=0, hbm=0, name=None, memory=24, scratch=(), cost=None):
    spaces = [pltpu.SMEM] * smem + [pltpu.VMEM] * n + [pltpu.HBM] * hbm
    vm = pl.BlockSpec(memory_space=pltpu.VMEM)
    return pl.pallas_call(
        kernel,
        out_shape=out_shape,
        in_specs=[pl.BlockSpec(memory_space=space) for space in spaces],
        out_specs=jax.tree.map(lambda _: vm, out_shape),
        scratch_shapes=scratch,
        compiler_params=pltpu.CompilerParams(vmem_limit_bytes=memory << 20),
        cost_estimate=cost,
        name=name,
    )


def shape(dims, dtype):
    return jax.ShapeDtypeStruct(dims, dtype)


def shards(queries, keys_new, values_new, cache_keys, cache_values, block_list, block_count, out_weight):
    ctx, head = lax.axis_index("ctx"), lax.axis_index("head")
    x, z = ctx // (NY * NZ), ctx % NZ
    core, half = head % CORES, head // CORES
    sel = block_list.shape[2]

    rows = cache_keys.shape[0]
    asked, kv = call(
        pack_kernel,
        (shape((queries.shape[0] + 8, queries.shape[1]), BF), shape((2 * rows, cache_keys.shape[1]), BF)),
        hbm=4,
        name="pack",
        scratch=[
            pltpu.VMEM(cache_values.shape, BF),
            pltpu.VMEM(block_list.shape, jnp.int32),
            pltpu.SemaphoreType.DMA((4,)),
        ],
    )(*(pltpu.with_memory_space_constraint(a, pltpu.HBM) for a in (block_list, queries, cache_keys, cache_values)))
    asked_pair = jnp.stack([asked, send(asked, PAIRS_Y)])
    after, before = send(kv, pairs_along(-1, True)), send(kv, pairs_along(1, True))
    asked_all = [asked_pair] + [send(asked_pair, pairs_along(-d, False)) for d in STEPS]
    half_keys, half_values = after[:rows], before[rows:]
    prev = send(jnp.concatenate([keys_new, values_new], axis=1), PAIRS_PREV)
    asked_pair, half_keys, half_values, prev = lax.optimization_barrier((asked_pair, half_keys, half_values, prev))
    far_keys = send(half_keys, pairs_along(-1, True))
    far_values = send(half_values, pairs_along(1, True))

    steps = jnp.array((0,) + STEPS, jnp.int32)
    owners = jnp.where(core == 0, ctx - z + (z + steps) % NZ, ctx + ((x + steps) % NX - x) * NY * NZ)

    def begin(asked, turn):
        lists = jnp.stack([a[:, BLOCK : BLOCK + KVL, None, :sel] for a in asked]).astype(jnp.int32)
        inside = lists // CB_DEV == owners[:, None]
        slot = lists % CB_DEV
        table = jnp.stack(
            [jnp.min(jnp.where(inside, slot, CB_DEV), axis=-1), jnp.max(jnp.where(inside, slot, -1), axis=-1)], axis=-1
        )
        table = jnp.clip(table, 0, CB_DEV - 1)
        n = len(asked)
        *begun, turn = call(
            functools.partial(early_kernel, n),
            (shape((NY, KVL, HD, COLS), F32), shape((NY, KVL, 8, COLS), F32)) * n + (shape((8, HD), F32),),
            smem=1,
            n=4 + n,
            name="early",
            cost=pl.CostEstimate(flops=0, transcendentals=0, bytes_accessed=1024),
        )(table, turn, kv, after, before, *asked)
        return [(table[i], asked[i], *begun[2 * i : 2 * i + 2]) for i in range(n)], turn

    begun, turn = begin([asked_pair], jnp.zeros((8, HD), F32))
    rest, turn = lax.optimization_barrier((asked_all[1:], turn))
    ended, turn = begin(rest, turn)
    begun = begun + ended

    parts = []
    for group in ((3, 1), (2, 0)):
        inputs = [a for i in group for a in begun[i][1:]]
        partials = call(
            functools.partial(late_kernel, len(group)),
            (shape((NY, KVL, ROWS, COLS), BF),) * len(group),
            smem=1,
            n=2 + len(inputs),
            name="late",
            cost=COST,
        )(jnp.stack([begun[i][0] for i in group]), far_keys, far_values, *inputs)
        parts += [p if i == 0 else send(p, pairs_along(((0,) + STEPS)[i], False)) for i, p in zip(group, partials)]
    other = call(functools.partial(join_kernel, 1), shape((KVL, ROWS, COLS), BF), n=4, name="join")(*parts)
    local = call(
        stretch_kernel, (shape((KVL, HD, COLS), F32), shape((KVL, 8, COLS), F32)), smem=1, n=4, name="stretch"
    )(jnp.minimum(ctx, 1).reshape(1), queries, keys_new, values_new, prev)
    other = send(other, PAIRS_Y)
    *home, weight = call(
        home_kernel,
        (
            shape((KVL, HD, COLS), F32),
            shape((KVL, 8, COLS), F32),
            shape(out_weight.shape, BF),
        ),
        n=6,
        hbm=1,
        name="home",
        scratch=[pltpu.SemaphoreType.DMA],
        memory=16,
        cost=COST,
    )(*parts, *local, pltpu.with_memory_space_constraint(out_weight, pltpu.HBM))

    share, width = BLOCK // (HALVES * CORES), out_weight.shape[1]
    theirs, mine = call(
        last_kernel,
        (shape((HALVES, share, width), BF), shape((HALVES, share, width), F32)),
        smem=1,
        n=4,
        name="last",
        scratch=[pltpu.VMEM((BLOCK, KVL * COLS), BF)],
        memory=16,
    )(jnp.stack([half, core]), *home, other, weight)
    chip = mine + send(theirs, PAIRS_CORE).astype(F32)
    return (chip[1] + send(chip[0].astype(BF), PAIRS_LO).astype(F32)).astype(BF)


def solution(mesh):
    return jax.shard_map(
        shards,
        mesh=mesh,
        in_specs=(
            P("ctx", "head"),
            P("ctx", "head"),
            P("ctx", "head"),
            P("ctx", "head"),
            P("ctx", "head"),
            P("head", "ctx", None),
            P("head", "ctx"),
            P("head", None),
        ),
        out_specs=P(("ctx", "head"), None),
        check_vma=False,
    )
```

```python
import functools

import jax
import jax.numpy as jnp
from jax import lax
from jax.experimental import pallas as pl
from jax.experimental.pallas import tpu as pltpu
from jax.sharding import PartitionSpec as P

HD = 128
BLOCK = 128
CB_DEV = 8
KVL = 2
GROUP = 4
NX, NY, NZ = 4, 2, 4
HALVES, CORES = 2, 2
COLS = GROUP * BLOCK
ROWS = HD + 8
STEPS = (1, -1, 2)
SCALE = HD**-0.5
NEG = -1e30
AXES = ("ctx", "head")
COST = pl.CostEstimate(flops=1 << 31, transcendentals=1 << 20, bytes_accessed=12 << 20)
BF = jnp.bfloat16
F32 = jnp.float32


def flat(x, y, z, yl, c):
    return ((x * NY + y) * NZ + z) * (HALVES * CORES) + yl * CORES + c


def everyone():
    for x in range(NX):
        for y in range(NY):
            for z in range(NZ):
                for yl in range(HALVES):
                    for c in range(CORES):
                        yield x, y, z, yl, c


def moved(x, y, z, yl, c, by, keys):
    if (c == 0) == keys:
        return flat(x, y, (z + by) % NZ, yl, c)
    return flat((x + by) % NX, y, z, yl, c)


def pairs_along(by, keys):
    return [(flat(*d), moved(*d, by, keys)) for d in everyone()]


PAIRS_Y = [(flat(x, y, z, l, c), flat(x, 1 - y, z, l, c)) for x, y, z, l, c in everyone()]
PAIRS_CORE = [(flat(x, y, z, l, c), flat(x, y, z, l, 1 - c)) for x, y, z, l, c in everyone()]
PAIRS_LO = [(flat(x, y, z, l, c), flat(x, y, z, 1 - l, c)) for x, y, z, l, c in everyone()]
PAIRS_PREV = [
    (i * HALVES * CORES + h, (i + 1) * HALVES * CORES + h)
    for i in range(NX * NY * NZ - 1)
    for h in range(HALVES * CORES)
]


def send(array, pairs):
    return lax.ppermute(array, AXES, pairs)


def nt(a, b):
    return lax.dot_general(a, b, (((1,), (1,)), ((), ())), preferred_element_type=F32)


def nn(a, b):
    return lax.dot_general(a, b, (((1,), (0,)), ((), ())), preferred_element_type=F32)


def turned(block):
    return block.astype(F32).T.astype(BF)


def packed_sum(level):
    hi = level.astype(BF)
    rest = level - hi.astype(F32)
    mid = rest.astype(BF)
    low = (rest - mid.astype(F32)).astype(BF)
    return jnp.concatenate([hi.astype(F32), mid.astype(F32), low.astype(F32), jnp.zeros((5, COLS), F32)], axis=0).astype(BF)


def pack_kernel(list_ref, q_ref, k_ref, v_ref, asked_ref, kv_ref, v_buf, list_buf, sems):
    rows = k_ref.shape[0]
    copies = [
        pltpu.make_async_copy(q_ref, asked_ref.at[0:BLOCK], sems.at[0]),
        pltpu.make_async_copy(v_ref, v_buf, sems.at[1]),
        pltpu.make_async_copy(k_ref, kv_ref.at[0:rows], sems.at[2]),
        pltpu.make_async_copy(list_ref, list_buf, sems.at[3]),
    ]
    for copy in copies:
        copy.start()
    asked_ref[BLOCK : BLOCK + 8, :] = jnp.zeros((8, asked_ref.shape[1]), BF)
    copies[3].wait()
    for h in range(KVL):
        asked_ref[BLOCK + h : BLOCK + h + 1, 0 : list_ref.shape[2]] = list_buf[h].astype(F32).astype(BF)
    copies[1].wait()
    for b in range(CB_DEV):
        for h in range(KVL):
            cols = slice(h * HD, (h + 1) * HD)
            kv_ref[rows + b * BLOCK : rows + (b + 1) * BLOCK, cols] = turned(v_buf[b * BLOCK : (b + 1) * BLOCK, cols])
    copies[0].wait()
    copies[2].wait()


def query_rows(q):
    return jnp.concatenate([q[:, m * HD : (m + 1) * HD] for m in range(GROUP)], axis=0)


def attend(tab_ref, q_ref, kvs, shard, y, h):
    q = query_rows(q_ref[y, 0:BLOCK, h * COLS : (h + 1) * COLS])
    cols = slice(h * HD, (h + 1) * HD)
    scores, offs, values = [], [], []
    for s, (keys, turned_values, base) in enumerate(kvs):
        first, second = tab_ref[y, h, shard + s, 0], tab_ref[y, h, shard + s, 1]
        for j, b in enumerate((first, second)):
            row = pl.multiple_of(b * BLOCK, BLOCK)
            scores.append(keys[pl.ds(row, BLOCK), cols])
            values.append(turned_values[pl.ds(row + base, BLOCK), cols])
            offs.append(None if j == 0 else jnp.where(second == first, NEG, 0.0).astype(F32))
    scores = nt(jnp.concatenate(scores, axis=0), q)
    scores = [scores[i * BLOCK : (i + 1) * BLOCK] for i in range(len(offs))]
    tops = [
        jnp.max(t, axis=0, keepdims=True) if o is None else jnp.max(t, axis=0, keepdims=True) + o
        for t, o in zip(scores, offs)
    ]
    top = functools.reduce(jnp.maximum, tops) * SCALE
    weights = [jnp.exp(t * SCALE - (top if o is None else top - o)).astype(BF) for t, o in zip(scores, offs)]
    weights = jnp.concatenate(weights, axis=0)
    ones = jnp.ones((8, weights.shape[0]), BF)
    mixture = nn(jnp.concatenate([jnp.concatenate(values, axis=1), ones], axis=0), weights)
    return top, mixture[HD : HD + 1], mixture[0:HD]


def early_kernel(count, tab_ref, turn_ref, kv0_ref, kv1_ref, kv2_ref, *refs):
    kvs = [(r, r, CB_DEV * BLOCK) for r in (kv0_ref, kv1_ref, kv2_ref)]
    refs[-1][...] = turn_ref[...]
    for i, q_ref in enumerate(refs[:count]):
        o_ref, s_ref = refs[count + 2 * i : count + 2 * i + 2]
        for y in range(NY):
            for h in range(KVL):
                top, total, mixture = attend(tab_ref.at[i], q_ref, kvs, 0, y, h)
                o_ref[y, h] = mixture
                s_ref[y, h, 0:1, :] = top
                s_ref[y, h, 1:2, :] = total


def late_kernel(count, tab_ref, k3_ref, v3_ref, *refs):
    kvs = [(k3_ref, v3_ref, 0)]
    inputs, outputs = refs[: 3 * count], refs[3 * count :]
    for i, o_ref in enumerate(outputs):
        q_ref, m_ref, s_ref = inputs[3 * i : 3 * i + 3]
        for y in range(NY):
            for h in range(KVL):
                top, total, mixture = attend(tab_ref.at[i], q_ref, kvs, 3, y, h)
                top0, total0 = s_ref[y, h, 0:1, :], s_ref[y, h, 1:2, :]
                peak = jnp.maximum(top, top0)
                share, share0 = jnp.exp(top - peak), jnp.exp(top0 - peak)
                total = total * share + total0 * share0
                inverse = 1.0 / total
                o_ref[y, h, 0:HD, :] = (mixture * (share * inverse) + m_ref[y, h] * (share0 * inverse)).astype(BF)
                o_ref[y, h, HD:ROWS, :] = packed_sum(peak + jnp.log(total))


def stretch_kernel(first_ref, q_ref, k_ref, v_ref, prev_ref, o_ref, l_ref):
    off = jnp.where(first_ref[0] == 0, NEG, 0.0).astype(F32)
    key = lax.broadcasted_iota(jnp.int32, (BLOCK, COLS), 0)
    row = lax.broadcasted_iota(jnp.int32, (BLOCK, COLS), 1) % BLOCK
    for h in range(KVL):
        q = query_rows(q_ref[:, h * COLS : (h + 1) * COLS])
        cols = slice(h * HD, (h + 1) * HD)
        vcols = slice((KVL + h) * HD, (KVL + h + 1) * HD)
        own = jnp.where(key <= row, nt(k_ref[:, cols], q), NEG)
        before = nt(prev_ref[:, cols], q)
        top = jnp.maximum(
            jnp.max(own, axis=0, keepdims=True), jnp.max(before, axis=0, keepdims=True) + off
        ) * SCALE
        w_own = jnp.exp(own * SCALE - top)
        w_before = jnp.exp(before * SCALE - (top - off))
        total = jnp.sum(w_own, axis=0, keepdims=True) + jnp.sum(w_before, axis=0, keepdims=True)
        mixture = nn(turned(v_ref[:, cols]), w_own.astype(BF)) + nn(
            turned(prev_ref[:, vcols]), w_before.astype(BF)
        )
        o_ref[h] = mixture * (1.0 / total)
        l_ref[h] = jnp.broadcast_to(top + jnp.log(total), (8, COLS))


def level_of(rows):
    r = rows.astype(F32)
    return r[0:1] + r[1:2] + r[2:3]


def joined(mixtures, levels):
    top = functools.reduce(jnp.maximum, levels)
    shares = [jnp.exp(v - top) for v in levels]
    total = functools.reduce(jnp.add, shares)
    inverse = 1.0 / total
    mixture = functools.reduce(jnp.add, [m * (s * inverse) for m, s in zip(mixtures, shares)])
    return mixture, top + jnp.log(total)


def join_kernel(which, *refs):
    parts, o_ref = refs[:-1], refs[-1]
    for h in range(KVL):
        mixture, level = joined(
            [p[which, h, 0:HD, :].astype(F32) for p in parts], [level_of(p[which, h, HD:ROWS, :]) for p in parts]
        )
        o_ref[h, 0:HD, :] = mixture.astype(BF)
        o_ref[h, HD:ROWS, :] = packed_sum(level)


def home_kernel(a_ref, b_ref, c_ref, d_ref, s_ref, l_ref, w_ref, o_ref, v_ref, copy_ref, sem):
    copy = pltpu.make_async_copy(w_ref, copy_ref, sem)
    copy.start()
    parts = (a_ref, b_ref, c_ref, d_ref)
    for h in range(KVL):
        mixtures = [p[0, h, 0:HD, :].astype(F32) for p in parts] + [s_ref[h]]
        levels = [level_of(p[0, h, HD:ROWS, :]) for p in parts] + [l_ref[h, 0:1, :]]
        mixture, level = joined(mixtures, levels)
        o_ref[h] = mixture
        v_ref[h] = jnp.broadcast_to(level, (8, COLS))
    copy.wait()


def last_kernel(place_ref, m_ref, v_ref, e_ref, w_ref, theirs_ref, mine_ref, att_ref):
    for h in range(KVL):
        mixture, _ = joined(
            [m_ref[h], e_ref[h, 0:HD, :].astype(F32)], [v_ref[h, 0:1, :], level_of(e_ref[h, HD:ROWS, :])]
        )
        for m in range(GROUP):
            c = (h * GROUP + m) * HD
            att_ref[:, c : c + HD] = mixture[:, m * BLOCK : (m + 1) * BLOCK].T.astype(BF)
    half, core = place_ref[0], place_ref[1]
    share = BLOCK // (HALVES * CORES)
    order = [(1 - half, 1 - core), (half, 1 - core), (1 - half, core), (half, core)]
    rows = [att_ref[pl.ds(pl.multiple_of((a * CORES + b) * share, share), share), :] for a, b in order]
    rows = jnp.concatenate(rows, axis=0)
    for n in range(4):
        cols = slice(n * w_ref.shape[1] // 4, (n + 1) * w_ref.shape[1] // 4)
        product = nn(rows, w_ref[:, cols])
        for i in range(HALVES):
            theirs_ref[i, :, cols] = product[i * share : (i + 1) * share].astype(BF)
            mine_ref[i, :, cols] = product[(HALVES + i) * share : (HALVES + i + 1) * share]


def call(kernel, out_shape, smem=0, n=0, hbm=0, name=None, memory=24, scratch=(), cost=None):
    spaces = [pltpu.SMEM] * smem + [pltpu.VMEM] * n + [pltpu.HBM] * hbm
    vm = pl.BlockSpec(memory_space=pltpu.VMEM)
    return pl.pallas_call(
        kernel,
        out_shape=out_shape,
        in_specs=[pl.BlockSpec(memory_space=space) for space in spaces],
        out_specs=jax.tree.map(lambda _: vm, out_shape),
        scratch_shapes=scratch,
        compiler_params=pltpu.CompilerParams(vmem_limit_bytes=memory << 20),
        cost_estimate=cost,
        name=name,
    )


def shape(dims, dtype):
    return jax.ShapeDtypeStruct(dims, dtype)


def shards(queries, keys_new, values_new, cache_keys, cache_values, block_list, block_count, out_weight):
    ctx, head = lax.axis_index("ctx"), lax.axis_index("head")
    x, z = ctx // (NY * NZ), ctx % NZ
    core, half = head % CORES, head // CORES
    sel = block_list.shape[2]

    rows = cache_keys.shape[0]
    asked, kv = call(
        pack_kernel,
        (shape((queries.shape[0] + 8, queries.shape[1]), BF), shape((2 * rows, cache_keys.shape[1]), BF)),
        hbm=4,
        name="pack",
        scratch=[
            pltpu.VMEM(cache_values.shape, BF),
            pltpu.VMEM(block_list.shape, jnp.int32),
            pltpu.SemaphoreType.DMA((4,)),
        ],
    )(*(pltpu.with_memory_space_constraint(a, pltpu.HBM) for a in (block_list, queries, cache_keys, cache_values)))
    asked_pair = jnp.stack([asked, send(asked, PAIRS_Y)])
    after, before = send(kv, pairs_along(-1, True)), send(kv, pairs_along(1, True))
    asked_all = [asked_pair] + [send(asked_pair, pairs_along(-d, False)) for d in STEPS]
    half_keys, half_values = after[:rows], before[rows:]
    prev = send(jnp.concatenate([keys_new, values_new], axis=1), PAIRS_PREV)
    asked_pair, half_keys, half_values, prev = lax.optimization_barrier((asked_pair, half_keys, half_values, prev))
    far_keys = send(half_keys, pairs_along(-1, True))
    far_values = send(half_values, pairs_along(1, True))

    steps = jnp.array((0,) + STEPS, jnp.int32)
    owners = jnp.where(core == 0, ctx - z + (z + steps) % NZ, ctx + ((x + steps) % NX - x) * NY * NZ)

    def begin(asked, turn):
        lists = jnp.stack([a[:, BLOCK : BLOCK + KVL, None, :sel] for a in asked]).astype(jnp.int32)
        inside = lists // CB_DEV == owners[:, None]
        slot = lists % CB_DEV
        table = jnp.stack(
            [jnp.min(jnp.where(inside, slot, CB_DEV), axis=-1), jnp.max(jnp.where(inside, slot, -1), axis=-1)], axis=-1
        )
        table = jnp.clip(table, 0, CB_DEV - 1)
        n = len(asked)
        *begun, turn = call(
            functools.partial(early_kernel, n),
            (shape((NY, KVL, HD, COLS), F32), shape((NY, KVL, 8, COLS), F32)) * n + (shape((8, HD), F32),),
            smem=1,
            n=4 + n,
            name="early",
            cost=pl.CostEstimate(flops=0, transcendentals=0, bytes_accessed=1024),
        )(table, turn, kv, after, before, *asked)
        return [(table[i], asked[i], *begun[2 * i : 2 * i + 2]) for i in range(n)], turn

    begun, turn = begin([asked_pair], jnp.zeros((8, HD), F32))
    rest, turn = lax.optimization_barrier((asked_all[1:], turn))
    ended, turn = begin(rest, turn)
    begun = begun + ended

    parts = []
    for group in ((3, 1), (2, 0)):
        inputs = [a for i in group for a in begun[i][1:]]
        partials = call(
            functools.partial(late_kernel, len(group)),
            (shape((NY, KVL, ROWS, COLS), BF),) * len(group),
            smem=1,
            n=2 + len(inputs),
            name="late",
            cost=COST,
        )(jnp.stack([begun[i][0] for i in group]), far_keys, far_values, *inputs)
        parts += [p if i == 0 else send(p, pairs_along(((0,) + STEPS)[i], False)) for i, p in zip(group, partials)]
    other = call(functools.partial(join_kernel, 1), shape((KVL, ROWS, COLS), BF), n=4, name="join")(*parts)
    local = call(
        stretch_kernel, (shape((KVL, HD, COLS), F32), shape((KVL, 8, COLS), F32)), smem=1, n=4, name="stretch"
    )(jnp.minimum(ctx, 1).reshape(1), queries, keys_new, values_new, prev)
    other = send(other, PAIRS_Y)
    *home, weight = call(
        home_kernel,
        (
            shape((KVL, HD, COLS), F32),
            shape((KVL, 8, COLS), F32),
            shape(out_weight.shape, BF),
        ),
        n=6,
        hbm=1,
        name="home",
        scratch=[pltpu.SemaphoreType.DMA],
        memory=16,
        cost=COST,
    )(*parts, *local, pltpu.with_memory_space_constraint(out_weight, pltpu.HBM))

    share, width = BLOCK // (HALVES * CORES), out_weight.shape[1]
    theirs, mine = call(
        last_kernel,
        (shape((HALVES, share, width), BF), shape((HALVES, share, width), F32)),
        smem=1,
        n=4,
        name="last",
        scratch=[pltpu.VMEM((BLOCK, KVL * COLS), BF)],
        memory=16,
    )(jnp.stack([half, core]), *home, other, weight)
    chip = mine + send(theirs, PAIRS_CORE).astype(F32)
    return (chip[1] + send(chip[0].astype(BF), PAIRS_LO).astype(F32)).astype(BF)


def solution(mesh):
    return jax.shard_map(
        shards,
        mesh=mesh,
        in_specs=(
            P("ctx", "head"),
            P("ctx", "head"),
            P("ctx", "head"),
            P("ctx", "head"),
            P("ctx", "head"),
            P("head", "ctx", None),
            P("head", "ctx"),
            P("head", None),
        ),
        out_specs=P(("ctx", "head"), None),
        check_vma=False,
    )
```

```python
import functools

import jax
import jax.numpy as jnp
from jax import lax
from jax.experimental import pallas as pl
from jax.experimental.pallas import tpu as pltpu
from jax.sharding import PartitionSpec as P

HD = 128
BLOCK = 128
CB_DEV = 8
KVL = 2
GROUP = 4
NX, NY, NZ = 4, 2, 4
HALVES, CORES = 2, 2
COLS = GROUP * BLOCK
ROWS = HD + 8
STEPS = (1, -1, 2)
SCALE = HD**-0.5
NEG = -1e30
AXES = ("ctx", "head")
COST = pl.CostEstimate(flops=1 << 31, transcendentals=1 << 20, bytes_accessed=12 << 20)
BF = jnp.bfloat16
F32 = jnp.float32


def flat(x, y, z, yl, c):
    return ((x * NY + y) * NZ + z) * (HALVES * CORES) + yl * CORES + c


def everyone():
    for x in range(NX):
        for y in range(NY):
            for z in range(NZ):
                for yl in range(HALVES):
                    for c in range(CORES):
                        yield x, y, z, yl, c


def moved(x, y, z, yl, c, by, keys):
    if (c == 0) == keys:
        return flat(x, y, (z + by) % NZ, yl, c)
    return flat((x + by) % NX, y, z, yl, c)


def pairs_along(by, keys):
    return [(flat(*d), moved(*d, by, keys)) for d in everyone()]


PAIRS_Y = [(flat(x, y, z, l, c), flat(x, 1 - y, z, l, c)) for x, y, z, l, c in everyone()]
PAIRS_CORE = [(flat(x, y, z, l, c), flat(x, y, z, l, 1 - c)) for x, y, z, l, c in everyone()]
PAIRS_LO = [(flat(x, y, z, l, c), flat(x, y, z, 1 - l, c)) for x, y, z, l, c in everyone()]
PAIRS_PREV = [
    (i * HALVES * CORES + h, (i + 1) * HALVES * CORES + h)
    for i in range(NX * NY * NZ - 1)
    for h in range(HALVES * CORES)
]


def send(array, pairs):
    return lax.ppermute(array, AXES, pairs)


def nt(a, b):
    return lax.dot_general(a, b, (((1,), (1,)), ((), ())), preferred_element_type=F32)


def nn(a, b):
    return lax.dot_general(a, b, (((1,), (0,)), ((), ())), preferred_element_type=F32)


def turned(block):
    return block.astype(F32).T.astype(BF)


def packed_sum(level):
    hi = level.astype(BF)
    rest = level - hi.astype(F32)
    mid = rest.astype(BF)
    low = (rest - mid.astype(F32)).astype(BF)
    return jnp.concatenate([hi.astype(F32), mid.astype(F32), low.astype(F32), jnp.zeros((5, COLS), F32)], axis=0).astype(BF)


def pack_kernel(list_ref, q_ref, k_ref, v_ref, kn_ref, vn_ref, asked_ref, kv_ref, rows_ref, v_buf, list_buf, sems):
    rows = k_ref.shape[0]
    copies = [
        pltpu.make_async_copy(q_ref, asked_ref.at[0:BLOCK], sems.at[0]),
        pltpu.make_async_copy(v_ref, v_buf, sems.at[1]),
        pltpu.make_async_copy(k_ref, kv_ref.at[0:rows], sems.at[2]),
        pltpu.make_async_copy(list_ref, list_buf, sems.at[3]),
        pltpu.make_async_copy(kn_ref, rows_ref.at[:, 0 : KVL * HD], sems.at[4]),
        pltpu.make_async_copy(vn_ref, rows_ref.at[:, KVL * HD : 2 * KVL * HD], sems.at[5]),
    ]
    for copy in copies:
        copy.start()
    asked_ref[BLOCK : BLOCK + 8, :] = jnp.zeros((8, asked_ref.shape[1]), BF)
    copies[3].wait()
    for h in range(KVL):
        asked_ref[BLOCK + h : BLOCK + h + 1, 0 : list_ref.shape[2]] = list_buf[h].astype(F32).astype(BF)
    copies[1].wait()
    for b in range(CB_DEV):
        for h in range(KVL):
            cols = slice(h * HD, (h + 1) * HD)
            kv_ref[rows + b * BLOCK : rows + (b + 1) * BLOCK, cols] = turned(v_buf[b * BLOCK : (b + 1) * BLOCK, cols])
    copies[0].wait()
    copies[2].wait()
    copies[4].wait()
    copies[5].wait()


def query_rows(q):
    return jnp.concatenate([q[:, m * HD : (m + 1) * HD] for m in range(GROUP)], axis=0)


def attend(tab_ref, q_ref, kvs, shard, y, h):
    q = query_rows(q_ref[y, 0:BLOCK, h * COLS : (h + 1) * COLS])
    cols = slice(h * HD, (h + 1) * HD)
    scores, offs, values = [], [], []
    for s, (keys, turned_values, base) in enumerate(kvs):
        first, second = tab_ref[y, h, shard + s, 0], tab_ref[y, h, shard + s, 1]
        for j, b in enumerate((first, second)):
            row = pl.multiple_of(b * BLOCK, BLOCK)
            scores.append(keys[pl.ds(row, BLOCK), cols])
            values.append(turned_values[pl.ds(row + base, BLOCK), cols])
            offs.append(None if j == 0 else jnp.where(second == first, NEG, 0.0).astype(F32))
    scores = nt(jnp.concatenate(scores, axis=0), q)
    scores = [scores[i * BLOCK : (i + 1) * BLOCK] for i in range(len(offs))]
    tops = [
        jnp.max(t, axis=0, keepdims=True) if o is None else jnp.max(t, axis=0, keepdims=True) + o
        for t, o in zip(scores, offs)
    ]
    top = functools.reduce(jnp.maximum, tops) * SCALE
    weights = [jnp.exp(t * SCALE - (top if o is None else top - o)).astype(BF) for t, o in zip(scores, offs)]
    weights = jnp.concatenate(weights, axis=0)
    ones = jnp.ones((8, weights.shape[0]), BF)
    mixture = nn(jnp.concatenate([jnp.concatenate(values, axis=1), ones], axis=0), weights)
    return top, mixture[HD : HD + 1], mixture[0:HD]


def early_kernel(count, tab_ref, turn_ref, kv0_ref, kv1_ref, kv2_ref, *refs):
    kvs = [(r, r, CB_DEV * BLOCK) for r in (kv0_ref, kv1_ref, kv2_ref)]
    refs[-1][...] = turn_ref[...]
    for i, q_ref in enumerate(refs[:count]):
        o_ref, s_ref = refs[count + 2 * i : count + 2 * i + 2]
        for y in range(NY):
            for h in range(KVL):
                top, total, mixture = attend(tab_ref.at[i], q_ref, kvs, 0, y, h)
                o_ref[y, h] = mixture
                s_ref[y, h, 0:1, :] = top
                s_ref[y, h, 1:2, :] = total


def late_kernel(count, tab_ref, k3_ref, v3_ref, *refs):
    kvs = [(k3_ref, v3_ref, 0)]
    inputs, outputs = refs[: 3 * count], refs[3 * count :]
    for i, o_ref in enumerate(outputs):
        q_ref, m_ref, s_ref = inputs[3 * i : 3 * i + 3]
        for y in range(NY):
            for h in range(KVL):
                top, total, mixture = attend(tab_ref.at[i], q_ref, kvs, 3, y, h)
                top0, total0 = s_ref[y, h, 0:1, :], s_ref[y, h, 1:2, :]
                peak = jnp.maximum(top, top0)
                share, share0 = jnp.exp(top - peak), jnp.exp(top0 - peak)
                total = total * share + total0 * share0
                inverse = 1.0 / total
                o_ref[y, h, 0:HD, :] = (mixture * (share * inverse) + m_ref[y, h] * (share0 * inverse)).astype(BF)
                o_ref[y, h, HD:ROWS, :] = packed_sum(peak + jnp.log(total))


def stretch_kernel(first_ref, q_ref, k_ref, v_ref, prev_ref, o_ref, l_ref):
    off = jnp.where(first_ref[0] == 0, NEG, 0.0).astype(F32)
    key = lax.broadcasted_iota(jnp.int32, (BLOCK, COLS), 0)
    row = lax.broadcasted_iota(jnp.int32, (BLOCK, COLS), 1) % BLOCK
    for h in range(KVL):
        q = query_rows(q_ref[:, h * COLS : (h + 1) * COLS])
        cols = slice(h * HD, (h + 1) * HD)
        vcols = slice((KVL + h) * HD, (KVL + h + 1) * HD)
        own = jnp.where(key <= row, nt(k_ref[:, cols], q), NEG)
        before = nt(prev_ref[:, cols], q)
        top = jnp.maximum(
            jnp.max(own, axis=0, keepdims=True), jnp.max(before, axis=0, keepdims=True) + off
        ) * SCALE
        w_own = jnp.exp(own * SCALE - top)
        w_before = jnp.exp(before * SCALE - (top - off))
        total = jnp.sum(w_own, axis=0, keepdims=True) + jnp.sum(w_before, axis=0, keepdims=True)
        mixture = nn(turned(v_ref[:, cols]), w_own.astype(BF)) + nn(
            turned(prev_ref[:, vcols]), w_before.astype(BF)
        )
        o_ref[h] = mixture * (1.0 / total)
        l_ref[h] = jnp.broadcast_to(top + jnp.log(total), (8, COLS))


def level_of(rows):
    r = rows.astype(F32)
    return r[0:1] + r[1:2] + r[2:3]


def joined(mixtures, levels):
    top = functools.reduce(jnp.maximum, levels)
    shares = [jnp.exp(v - top) for v in levels]
    total = functools.reduce(jnp.add, shares)
    inverse = 1.0 / total
    mixture = functools.reduce(jnp.add, [m * (s * inverse) for m, s in zip(mixtures, shares)])
    return mixture, top + jnp.log(total)


def join_kernel(which, *refs):
    parts, o_ref = refs[:-1], refs[-1]
    for h in range(KVL):
        mixture, level = joined(
            [p[which, h, 0:HD, :].astype(F32) for p in parts], [level_of(p[which, h, HD:ROWS, :]) for p in parts]
        )
        o_ref[h, 0:HD, :] = mixture.astype(BF)
        o_ref[h, HD:ROWS, :] = packed_sum(level)


def home_kernel(a_ref, b_ref, c_ref, d_ref, s_ref, l_ref, w_ref, o_ref, v_ref, copy_ref, sem):
    copy = pltpu.make_async_copy(w_ref, copy_ref, sem)
    copy.start()
    parts = (a_ref, b_ref, c_ref, d_ref)
    for h in range(KVL):
        mixtures = [p[0, h, 0:HD, :].astype(F32) for p in parts] + [s_ref[h]]
        levels = [level_of(p[0, h, HD:ROWS, :]) for p in parts] + [l_ref[h, 0:1, :]]
        mixture, level = joined(mixtures, levels)
        o_ref[h] = mixture
        v_ref[h] = jnp.broadcast_to(level, (8, COLS))
    copy.wait()


def last_kernel(place_ref, m_ref, v_ref, e_ref, w_ref, theirs_ref, mine_ref, att_ref):
    for h in range(KVL):
        mixture, _ = joined(
            [m_ref[h], e_ref[h, 0:HD, :].astype(F32)], [v_ref[h, 0:1, :], level_of(e_ref[h, HD:ROWS, :])]
        )
        for m in range(GROUP):
            c = (h * GROUP + m) * HD
            att_ref[:, c : c + HD] = mixture[:, m * BLOCK : (m + 1) * BLOCK].T.astype(BF)
    half, core = place_ref[0], place_ref[1]
    share = BLOCK // (HALVES * CORES)
    order = [(1 - half, 1 - core), (half, 1 - core), (1 - half, core), (half, core)]
    rows = [att_ref[pl.ds(pl.multiple_of((a * CORES + b) * share, share), share), :] for a, b in order]
    rows = jnp.concatenate(rows, axis=0)
    for n in range(4):
        cols = slice(n * w_ref.shape[1] // 4, (n + 1) * w_ref.shape[1] // 4)
        product = nn(rows, w_ref[:, cols])
        for i in range(HALVES):
            theirs_ref[i, :, cols] = product[i * share : (i + 1) * share].astype(BF)
            mine_ref[i, :, cols] = product[(HALVES + i) * share : (HALVES + i + 1) * share]


def call(kernel, out_shape, smem=0, n=0, hbm=0, name=None, memory=24, scratch=(), cost=None):
    spaces = [pltpu.SMEM] * smem + [pltpu.VMEM] * n + [pltpu.HBM] * hbm
    vm = pl.BlockSpec(memory_space=pltpu.VMEM)
    return pl.pallas_call(
        kernel,
        out_shape=out_shape,
        in_specs=[pl.BlockSpec(memory_space=space) for space in spaces],
        out_specs=jax.tree.map(lambda _: vm, out_shape),
        scratch_shapes=scratch,
        compiler_params=pltpu.CompilerParams(vmem_limit_bytes=memory << 20),
        cost_estimate=cost,
        name=name,
    )


def shape(dims, dtype):
    return jax.ShapeDtypeStruct(dims, dtype)


def shards(queries, keys_new, values_new, cache_keys, cache_values, block_list, block_count, out_weight):
    ctx, head = lax.axis_index("ctx"), lax.axis_index("head")
    x, z = ctx // (NY * NZ), ctx % NZ
    core, half = head % CORES, head // CORES
    sel = block_list.shape[2]

    rows = cache_keys.shape[0]
    asked, kv, stretch_rows = call(
        pack_kernel,
        (
            shape((queries.shape[0] + 8, queries.shape[1]), BF),
            shape((2 * rows, cache_keys.shape[1]), BF),
            shape((BLOCK, 2 * KVL * HD), BF),
        ),
        hbm=6,
        name="pack",
        scratch=[
            pltpu.VMEM(cache_values.shape, BF),
            pltpu.VMEM(block_list.shape, jnp.int32),
            pltpu.SemaphoreType.DMA((6,)),
        ],
    )(*(pltpu.with_memory_space_constraint(a, pltpu.HBM) for a in (block_list, queries, cache_keys, cache_values, keys_new, values_new)))
    asked_pair = jnp.stack([asked, send(asked, PAIRS_Y)])
    after, before = send(kv, pairs_along(-1, True)), send(kv, pairs_along(1, True))
    asked_all = [asked_pair] + [send(asked_pair, pairs_along(-d, False)) for d in STEPS]
    half_keys, half_values = after[:rows], before[rows:]
    prev = send(stretch_rows, PAIRS_PREV)
    asked_pair, half_keys, half_values, prev = lax.optimization_barrier((asked_pair, half_keys, half_values, prev))
    far_keys = send(half_keys, pairs_along(-1, True))
    far_values = send(half_values, pairs_along(1, True))

    steps = jnp.array((0,) + STEPS, jnp.int32)
    owners = jnp.where(core == 0, ctx - z + (z + steps) % NZ, ctx + ((x + steps) % NX - x) * NY * NZ)

    def begin(asked, turn):
        lists = jnp.stack([a[:, BLOCK : BLOCK + KVL, None, :sel] for a in asked]).astype(jnp.int32)
        inside = lists // CB_DEV == owners[:, None]
        slot = lists % CB_DEV
        table = jnp.stack(
            [jnp.min(jnp.where(inside, slot, CB_DEV), axis=-1), jnp.max(jnp.where(inside, slot, -1), axis=-1)], axis=-1
        )
        table = jnp.clip(table, 0, CB_DEV - 1)
        n = len(asked)
        *begun, turn = call(
            functools.partial(early_kernel, n),
            (shape((NY, KVL, HD, COLS), F32), shape((NY, KVL, 8, COLS), F32)) * n + (shape((8, HD), F32),),
            smem=1,
            n=4 + n,
            name="early",
            cost=pl.CostEstimate(flops=0, transcendentals=0, bytes_accessed=1024),
        )(table, turn, kv, after, before, *asked)
        return [(table[i], asked[i], *begun[2 * i : 2 * i + 2]) for i in range(n)], turn

    begun, turn = begin([asked_pair], jnp.zeros((8, HD), F32))
    rest, turn = lax.optimization_barrier((asked_all[1:], turn))
    ended, turn = begin(rest, turn)
    begun = begun + ended

    parts = []
    for group in ((3, 1), (2, 0)):
        inputs = [a for i in group for a in begun[i][1:]]
        partials = call(
            functools.partial(late_kernel, len(group)),
            (shape((NY, KVL, ROWS, COLS), BF),) * len(group),
            smem=1,
            n=2 + len(inputs),
            name="late",
            cost=COST,
        )(jnp.stack([begun[i][0] for i in group]), far_keys, far_values, *inputs)
        parts += [p if i == 0 else send(p, pairs_along(((0,) + STEPS)[i], False)) for i, p in zip(group, partials)]
    other = call(functools.partial(join_kernel, 1), shape((KVL, ROWS, COLS), BF), n=4, name="join")(*parts)
    local = call(
        stretch_kernel, (shape((KVL, HD, COLS), F32), shape((KVL, 8, COLS), F32)), smem=1, n=4, name="stretch"
    )(jnp.minimum(ctx, 1).reshape(1), queries, keys_new, values_new, prev)
    other = send(other, PAIRS_Y)
    *home, weight = call(
        home_kernel,
        (
            shape((KVL, HD, COLS), F32),
            shape((KVL, 8, COLS), F32),
            shape(out_weight.shape, BF),
        ),
        n=6,
        hbm=1,
        name="home",
        scratch=[pltpu.SemaphoreType.DMA],
        memory=16,
        cost=COST,
    )(*parts, *local, pltpu.with_memory_space_constraint(out_weight, pltpu.HBM))

    share, width = BLOCK // (HALVES * CORES), out_weight.shape[1]
    theirs, mine = call(
        last_kernel,
        (shape((HALVES, share, width), BF), shape((HALVES, share, width), F32)),
        smem=1,
        n=4,
        name="last",
        scratch=[pltpu.VMEM((BLOCK, KVL * COLS), BF)],
        memory=16,
    )(jnp.stack([half, core]), *home, other, weight)
    chip = mine + send(theirs, PAIRS_CORE).astype(F32)
    return (chip[1] + send(chip[0].astype(BF), PAIRS_LO).astype(F32)).astype(BF)


def solution(mesh):
    return jax.shard_map(
        shards,
        mesh=mesh,
        in_specs=(
            P("ctx", "head"),
            P("ctx", "head"),
            P("ctx", "head"),
            P("ctx", "head"),
            P("ctx", "head"),
            P("head", "ctx", None),
            P("head", "ctx"),
            P("head", None),
        ),
        out_specs=P(("ctx", "head"), None),
        check_vma=False,
    )
```
